32 devices in a mesh: rows: 4 (over z), cols: 8 (over y, x, core).
Axes of the slice: x: 2, y: 2, z: 4, core: 2. Of those that a mesh axis runs over, the one named last changes fastest.
Arguments:
- right_side: float32 [256, 128, 256], P('rows', 'cols'), may hold values from -3 to 15
- initial: float32 [256, 128, 256], P('rows', 'cols'), may hold values from -0.15 to 2.15
- conduct: float32 [256, 128, 256], P('rows', 'cols'), may hold values from 0.5 to 2
Outputs:
- basis: float32 [5, 256, 128, 256], P(None, 'rows', 'cols')
- rfactor: float32 [5, 5], replicated
- updated: float32 [256, 128, 256], P('rows', 'cols')
The draws below stay inside these ranges and needn't reach their ends.
All inputs are finite; a program needn't handle non-finite values.
Results may differ from the reference program's by a relative error of at most 0.0028.
Values sent between devices are 32-bit elements; how exact they have to be, the bound alone decides.
A program may use at most 128 MiB of HBM per device.

```python
import math
import jax
import jax.numpy as jnp
import numpy as np
from jax import lax

CZ = 256
NX = 256
NY = 128


def smooth_profile():
    pos_x = (jnp.arange(NX, dtype=jnp.float32) + 0.5) / NX
    pos_y = (jnp.arange(NY, dtype=jnp.float32) + 0.5) / NY
    pos_z = (jnp.arange(CZ, dtype=jnp.float32) + 0.5) / CZ
    return jnp.sin(jnp.pi * pos_x)[:, None, None] * jnp.sin(jnp.pi * pos_y)[None, :, None] * jnp.sin(jnp.pi * pos_z)[None, None, :]


def draw_right_side(key, part):
    own_key = jax.random.fold_in(key, 11)
    height_key = jax.random.fold_in(own_key, 0)
    second_key = jax.random.fold_in(own_key, 2)
    height = jax.random.uniform(height_key, (), jnp.float32, 9.0, 12.0)
    pos_x = jnp.arange(NX, dtype=jnp.float32) / NX
    pos_y = jnp.arange(NY, dtype=jnp.float32) / NY
    amplitude = 10.0 ** (0.5 * (pos_x[:, None, None] + pos_y[None, :, None]) - 0.5)
    rough_part = 0.2 * jnp.clip(jax.random.normal(second_key, (NX, NY, CZ), jnp.float32), -4.0, 4.0)
    values = height * smooth_profile() + rough_part * amplitude
    return values.astype(jnp.float32)


def draw_initial(key, part):
    own_key = jax.random.fold_in(key, 23)
    height_key = jax.random.fold_in(own_key, 0)
    second_key = jax.random.fold_in(own_key, 2)
    height = jax.random.uniform(height_key, (), jnp.float32, 1.0, 2.0)
    rough_part = 0.035 * jnp.clip(jax.random.normal(second_key, (NX, NY, CZ), jnp.float32), -4.0, 4.0)
    values = height * smooth_profile() + rough_part
    return values.astype(jnp.float32)


def block_levels(key, dims, cuts, smallest, high):
    loudness = 1.0
    for position, parts in cuts:
        steps = jax.random.uniform(jax.random.fold_in(jax.random.fold_in(key, 6), position), (parts,), jnp.float32, smallest / len(cuts), high / len(cuts))
        loudness = loudness * jnp.repeat(jnp.exp(steps), dims[position] // parts).reshape((-1,) + (1,) * (len(dims) - 1 - position))
    return loudness


def setup_inputs(seed: int = 0) -> dict:
    key_list = jax.random.split(jax.random.key(seed), 4)
    return {
        "right_side": draw_right_side(jax.random.fold_in(key_list[3], 71), 0),
        "initial": draw_initial(jax.random.fold_in(key_list[3], 71), 0),
        "conduct": jnp.clip(jnp.exp(math.log(2.0) - 1.3862944 * jax.random.uniform(key_list[2], (NX, NY, CZ), jnp.float32) ** block_levels(key_list[2], (NX, NY, CZ), ((0, 4), (1, 8)), -0.2, 0.2)), 0.5, 2.0),
    }


newton_shifts = (12.0, 3.0, 21.0, 7.0)
newton_scales = (8.0, 8.0, 8.0, 8.0)

def stencil_apply(field, coeff):
    field_z = jnp.pad(field, ((0, 0), (0, 0), (1, 1)))
    coeff_z = jnp.pad(coeff, ((0, 0), (0, 0), (1, 1)))
    center = field[1:-1, 1:-1]
    center_k = coeff[1:-1, 1:-1]
    beside_all = [(field[2:, 1:-1], coeff[2:, 1:-1]), (field[:-2, 1:-1], coeff[:-2, 1:-1]), (field[1:-1, 2:], coeff[1:-1, 2:]), (field[1:-1, :-2], coeff[1:-1, :-2]), (field_z[1:-1, 1:-1, 2:], coeff_z[1:-1, 1:-1, 2:]), (field_z[1:-1, 1:-1, :-2], coeff_z[1:-1, 1:-1, :-2])]
    total = jnp.zeros(center.shape, center.dtype)
    for other, other_k in beside_all:
        total = total + 0.5 * (center_k + other_k) * (center - other)
    return total

def padded(array):
    return jnp.pad(array, ((1, 1), (1, 1), (0, 0)))

def small_cholesky(matrix):
    order = matrix.shape[0]
    zero_val = matrix[0, 0] * 0.0
    lower = [[zero_val for col in range(order)] for row in range(order)]
    for col in range(order):
        diag_val = matrix[col, col]
        for inner in range(col):
            diag_val = diag_val - lower[col][inner] * lower[col][inner]
        lower[col][col] = jnp.sqrt(diag_val)
        for row in range(col + 1, order):
            entry = matrix[row, col]
            for inner in range(col):
                entry = entry - lower[row][inner] * lower[col][inner]
            lower[row][col] = entry / lower[col][col]
    return jnp.stack([jnp.stack(line) for line in lower])

def lower_inverse(lower):
    order = lower.shape[0]
    ident = jnp.eye(order, dtype=lower.dtype)
    result_rows = []
    for row in range(order):
        entry = ident[row]
        for inner in range(row):
            entry = entry - lower[row, inner] * result_rows[inner]
        result_rows.append(entry / lower[row, row])
    return jnp.stack(result_rows)

def upper_inverse(upper):
    order = upper.shape[0]
    ident = jnp.eye(order, dtype=upper.dtype)
    result_rows = [None] * order
    for row in range(order - 1, -1, -1):
        entry = ident[row]
        for inner in range(row + 1, order):
            entry = entry - upper[row, inner] * result_rows[inner]
        result_rows[row] = entry / upper[row, row]
    return jnp.stack(result_rows)

def gram_of(stacked):
    return lax.dot_general(stacked, stacked, (((1,), (1,)), ((), ())), precision=lax.Precision.HIGHEST)

def least_squares(rfactor):
    table = np.zeros((5, 4))
    for step in range(4):
        table[step, step] = newton_shifts[step]
        table[step + 1, step] = newton_scales[step]
    change = jnp.asarray(table, dtype=rfactor.dtype)
    upper_inv = upper_inverse(rfactor[:4, :4])
    hess = jnp.dot(jnp.dot(rfactor, change, precision=lax.Precision.HIGHEST), upper_inv, precision=lax.Precision.HIGHEST)
    normal_mat = jnp.dot(hess.T, hess, precision=lax.Precision.HIGHEST)
    target = rfactor[0, 0] * hess[0, :]
    factor_inv = lower_inverse(small_cholesky(normal_mat))
    middle = jnp.dot(factor_inv, target, precision=lax.Precision.HIGHEST)
    return jnp.dot(factor_inv.T, middle, precision=lax.Precision.HIGHEST)

def reference(right_side, initial, conduct):
    coeff_pad = padded(conduct)
    residual = right_side - stencil_apply(padded(initial), coeff_pad)
    vectors = [residual]
    for step in range(4):
        current = vectors[-1]
        vectors.append((stencil_apply(padded(current), coeff_pad) - newton_shifts[step] * current) / newton_scales[step])
    stacked = jnp.stack(vectors).reshape(5, -1)
    lower_one = small_cholesky(gram_of(stacked))
    first_q = jnp.dot(lower_inverse(lower_one), stacked, precision=lax.Precision.HIGHEST)
    lower_two = small_cholesky(gram_of(first_q))
    final_q = jnp.dot(lower_inverse(lower_two), first_q, precision=lax.Precision.HIGHEST)
    rfactor = jnp.dot(lower_two.T, lower_one.T, precision=lax.Precision.HIGHEST)
    weights = least_squares(rfactor)
    updated = initial + jnp.dot(weights, final_q[:4], precision=lax.Precision.HIGHEST).reshape(initial.shape)
    count = initial.shape[0] * initial.shape[1] * initial.shape[2]
    basis = (final_q * jnp.sqrt(jnp.float32(count)).astype(final_q.dtype)).reshape((5,) + initial.shape)
    return (basis, rfactor, updated)
```

```python
import functools
import math

import jax
import jax.numpy as jnp
from jax import lax
from jax.experimental import pallas as pl
from jax.experimental.pallas import tpu as pltpu
from jax.sharding import PartitionSpec as P

SHIFTS = (12.0, 3.0, 21.0, 7.0)
NEWTON = (0.0,) + SHIFTS[:3]
SCALE = 8.0
LANES = 128
MESH = pl.DeviceIdType.MESH
PAIRS = [(i, j) for j in range(5) for i in range(j + 1)]
F32 = jnp.float32


def inv_sqrt(value):
    guess = lax.rsqrt(value)
    return guess * (1.5 - 0.5 * (value * guess) * guess)


def cholesky(entry, order):
    lower, inv = {}, []
    for col in range(order):
        diag = entry(col, col)
        for inner in range(col):
            diag = diag - lower[col, inner] * lower[col, inner]
        root = inv_sqrt(diag)
        inv.append(root)
        lower[col, col] = diag * root
        for row in range(col + 1, order):
            val = entry(row, col)
            for inner in range(col):
                val = val - lower[row, inner] * lower[col, inner]
            lower[row, col] = val * root
    return lower, inv


def lower_inverse(lower, inv, order):
    result = {}
    for row in range(order):
        for col in range(row):
            total = lower[row, col] * result[col, col]
            for inner in range(col + 1, row):
                total = total + lower[row, inner] * result[inner, col]
            result[row, col] = -(total * inv[row])
        result[row, row] = inv[row]
    return result


def cycle_kernel(sizes, rs_hbm, init_hbm, cond_hbm, v_out, coef_out,
                 ku, rs, v0, v1, v2, v3, v4, cx, cy, cyb, cz, czb, cfx, cfy, fy, hx, hy,
                 g1, g2, gm, load_sem, out_sem, hs_sem, hr_sem, s1, r1, s2, r2):
    nrows, ncols, nx, ny, nz = sizes
    nh = nz // LANES
    count = nx * ny
    step_rows = 4 * ny
    one_stage = nrows * ncols <= 64
    vecs = (v0, v1, v2, v3, v4)
    me_r, me_c = lax.axis_index("rows"), lax.axis_index("cols")

    loads = []
    for idx, (src, dst) in enumerate(((cond_hbm, ku.at[0]), (init_hbm, ku.at[1]), (rs_hbm, rs))):
        for h in range(nh):
            loads.append(pltpu.make_async_copy(
                src.at[:, pl.ds(h * LANES, LANES)], dst.at[h, pl.ds(0, count), :],
                load_sem.at[idx, h]))
            loads[-1].start()

    barrier = pltpu.get_barrier_semaphore()
    everyone = [(dr, dc) for dr in range(nrows) for dc in range(ncols)][1:]
    greeted = everyone if one_stage else (
        [(0, d) for d in range(1, ncols)] + [(d, 0) for d in range(1, nrows)])
    for dr, dc in greeted:
        pl.semaphore_signal(barrier, inc=1, device_id_type=MESH,
                            device_id=(lax.rem(me_r + dr, nrows), lax.rem(me_c + dc, ncols)))

    zero_plane = jnp.zeros((nh, ny, LANES), F32)
    for i in range(2):
        ku[i, :, pl.ds(count, ny), :] = zero_plane
    for vec in vecs[:4]:
        vec[:, pl.ds(count, ny), :] = zero_plane
    for edge, ref, side in ((me_c == 0, hy, 0), (me_c == ncols - 1, hy, 1),
                            (me_r == 0, hx, 0), (me_r == nrows - 1, hx, 1)):
        @pl.when(edge)
        def _(ref=ref, side=side):
            for k in range(6):
                ref[k, side] = jnp.zeros(ref.shape[2:], F32)

    def strided(side):
        return pl.ds(0 if side == 0 else ny - 1, nx, stride=ny)

    def face_copies(first, num, plane):
        made = []
        ks = first if num is None else pl.ds(first, num)
        for slot, axis, me, size in ((0, "cols", me_c, ncols), (1, "cols", me_c, ncols),
                                     (2, "rows", me_r, nrows), (3, "rows", me_r, nrows)):
            side = slot % 2
            target = me + 1 if side == 0 else me - 1
            has_target = me < size - 1 if side == 0 else me > 0
            has_source = me > 0 if side == 0 else me < size - 1
            if axis == "cols":
                src, dst = fy.at[ks, 1 - side], hy.at[ks, side]
            else:
                src, dst = plane(1 - side), hx.at[ks, side]
            made.append((has_target, has_source, pltpu.make_async_remote_copy(
                src_ref=src, dst_ref=dst, send_sem=hs_sem.at[first, slot],
                recv_sem=hr_sem.at[first, slot], device_id={axis: target}, device_id_type=MESH)))
        return made

    sent = []

    def send(copies):
        sent.extend(copies)
        for has_target, _, copy in copies:
            @pl.when(has_target)
            def _(copy=copy):
                copy.start()

    def arrive(copies):
        for _, has_source, copy in copies:
            @pl.when(has_source)
            def _(copy=copy):
                copy.wait_recv()

    def plane_start(side):
        return 0 if side == 0 else count - ny

    for cp in loads[:2 * nh]:
        cp.wait()
    for i in range(2):
        for side in range(2):
            for h in range(nh):
                fy[i, side, h] = ku[i, h, strided(side), :]
    pl.semaphore_wait(barrier, len(greeted))
    first = face_copies(0, 2, lambda side: ku.at[:, :, pl.ds(plane_start(side), ny), :])
    send(first)

    def wide(ref, base, rows):
        return jnp.concatenate([ref[h, pl.ds(base, rows), :] for h in range(nh)], axis=1)

    def put(ref, base, rows, value):
        for h in range(nh):
            ref[h, pl.ds(base, rows), :] = value[:, h * LANES:(h + 1) * LANES]

    lane = lax.broadcasted_iota(jnp.int32, (step_rows, nz), 1)
    row = lax.broadcasted_iota(jnp.int32, (step_rows, nz), 0)
    sixteenth = 0.5 / SCALE
    y_mask = jnp.where(lax.rem(row, ny) == ny - 1, 0.0, sixteenth).astype(F32)
    z_mask = jnp.where(lane == nz - 1, 0.0, sixteenth).astype(F32)
    z_edge = jnp.where((lane == nz - 1) | (lane == 0), sixteenth, 0.0).astype(F32)
    kk, uu = ku.at[0], ku.at[1]

    @pl.loop(0, count // step_rows)
    def _(i):
        base = pl.multiple_of(i * step_rows, step_rows)
        here = wide(kk, base, step_rows)
        put(cx, base, step_rows, (here + wide(kk, base + ny, step_rows)) * sixteenth)
        above = (here + pltpu.roll(here, step_rows - 1, 0)) * y_mask
        put(cy, base, step_rows, above)
        put(cyb, base, step_rows, pltpu.roll(above, 1, 0))
        after = (here + pltpu.roll(here, nz - 1, 1)) * z_mask
        put(cz, base, step_rows, after)
        put(czb, base, step_rows, pltpu.roll(after, 1, 1))
    cx[:, pl.ds(count - ny, ny), :] = zero_plane

    def interior(src, dst, shift, residual):
        def body(i, flux_before):
            base = pl.multiple_of(i * step_rows, step_rows)
            val = wide(src, base, step_rows)
            flux_x = wide(cx, base, step_rows) * (val - wide(src, base + ny, step_rows))
            total = flux_x - jnp.concatenate([flux_before, flux_x[:step_rows - ny]], axis=0)
            total = total + wide(cy, base, step_rows) * (val - pltpu.roll(val, step_rows - 1, 0))
            total = total + wide(cyb, base, step_rows) * (val - pltpu.roll(val, 1, 0))
            total = total + wide(cz, base, step_rows) * (val - pltpu.roll(val, nz - 1, 1))
            total = total + wide(czb, base, step_rows) * (val - pltpu.roll(val, 1, 1))
            total = total + (wide(kk, base, step_rows) * z_edge - shift) * val
            if residual:
                total = wide(rs, base, step_rows) - SCALE * total
            put(dst, base, step_rows, total)
            return flux_x[step_rows - ny:]
        lax.fori_loop(0, count // step_rows, body, jnp.zeros((ny, nz), F32))

    def corrections(k, src, dst, sign, pack):
        for side in range(2):
            at = pl.ds(plane_start(side), ny)
            dst[:, at, :] = dst[:, at, :] + sign * (cfx[side] * (src[:, at, :] - hx[k, side]))
        for side in range(2):
            for h in range(nh):
                new = dst[h, strided(side), :] + sign * (
                    cfy[side, h] * (fy[k, side, h] - hy[k, side, h]))
                dst[h, strided(side), :] = new
                if pack:
                    fy[k + 1, side, h] = new

    for cp in loads[2 * nh:]:
        cp.wait()
    interior(uu, v0, 0.0, True)
    arrive(first)
    for side in range(2):
        at = pl.ds(plane_start(side), ny)
        cfx[side] = (kk[:, at, :] + hx[0, side]) * sixteenth
        cfy[side] = (fy[0, side] + hy[0, side]) * sixteenth
    corrections(1, uu, v0, -SCALE, True)

    sums = {}

    def gram_with(k):
        def body(i, accs):
            base = pl.multiple_of(i * 16, 16)
            accs = list(accs)
            for h in range(nh):
                for sub in range(2):
                    at = pl.ds(base + 8 * sub, 8)
                    mine = vecs[k][h, at, :]
                    for j in range(k + 1):
                        other = mine if j == k else vecs[j][h, at, :]
                        accs[j] = accs[j] + mine * other
            return tuple(accs)
        accs = lax.fori_loop(0, count // 16, body,
                             tuple(jnp.zeros((8, LANES), F32) for _ in range(k + 1)), unroll=2)
        for j in range(k + 1):
            sums[j, k] = accs[j]

    outs = []

    def write_out(k):
        for h in range(nh):
            outs.append(pltpu.make_async_copy(
                (vecs[k] if k < 5 else uu).at[h, pl.ds(0, count), :], v_out.at[k, :, pl.ds(h * LANES, LANES)],
                out_sem.at[k, h]))
            outs[-1].start()

    write_out(5)
    for k in range(4):
        vec = vecs[k]
        copies = face_copies(2 + k, None,
                             lambda side, vec=vec: vec.at[:, pl.ds(plane_start(side), ny), :])
        send(copies)
        write_out(k)
        interior(vec, vecs[k + 1], NEWTON[k] / SCALE, False)
        gram_with(k)
        arrive(copies)
        corrections(2 + k, vec, vecs[k + 1], 1.0, k < 3)
    write_out(4)
    gram_with(4)

    def exchange(p, buf, ssem, rsem, peers, slot, value):
        buf[p, slot(0, 0)] = value
        for e, (dr, dc) in enumerate(peers):
            copy = pltpu.make_async_remote_copy(
                src_ref=buf.at[p, slot(0, 0)], dst_ref=buf.at[p, slot(0, 0)],
                send_sem=ssem.at[p, e], recv_sem=rsem.at[p, e],
                device_id=(lax.rem(me_r + dr, nrows), lax.rem(me_c + dc, ncols)),
                device_id_type=MESH)
            copy.start()
            sent.append((None, None, copy))
        for e, (dr, dc) in enumerate(peers):
            pltpu.make_async_remote_copy(
                src_ref=buf.at[p, slot(0, 0)], dst_ref=buf.at[p, slot(nrows - dr, ncols - dc)],
                send_sem=ssem.at[p, e], recv_sem=rsem.at[p, e],
                device_id=(lax.rem(me_r + nrows - dr, nrows), lax.rem(me_c + ncols - dc, ncols)),
                device_id_type=MESH).wait_recv()
        parts = [buf[p, i] for i in range(len(peers) + 1)]
        while len(parts) > 1:
            parts = [a + b for a, b in zip(parts[::2], parts[1::2])] + (
                parts[-1:] if len(parts) % 2 else [])
        return parts[0]

    def col_of(dc):
        return lax.rem(me_c + dc, ncols)

    def row_of(dr):
        return lax.rem(me_r + dr, nrows)

    pair_row = lax.broadcasted_iota(jnp.int32, (16, LANES), 0)
    on_diag = pair_row == lax.broadcasted_iota(jnp.int32, (16, LANES), 1)

    def all_reduce(p, values):
        for e, pair in enumerate(PAIRS):
            gm[e:e + 1, :] = jnp.sum(values[pair], axis=0, keepdims=True)
        line = jnp.sum(jnp.where(on_diag, jnp.sum(gm[...], axis=1, keepdims=True), 0.0),
                       axis=0, keepdims=True)
        if one_stage:
            line = exchange(p, g1, s1, r1, everyone,
                            lambda dr, dc: row_of(dr) * ncols + col_of(dc), line)
        else:
            line = exchange(p, g1, s1, r1, [(0, d) for d in range(1, ncols)],
                            lambda dr, dc: col_of(dc), line)
            line = exchange(p, g2, s2, r2, [(d, 0) for d in range(1, nrows)],
                            lambda dr, dc: row_of(dr), line)
        gm[...] = jnp.broadcast_to(
            jnp.sum(jnp.where(on_diag, line, 0.0), axis=1, keepdims=True), gm.shape)
        full = {pair: gm[e:e + 1, :] for e, pair in enumerate(PAIRS)}
        return lambda i, j: full[min(i, j), max(i, j)]

    def add_up(terms):
        return functools.reduce(lambda a, b: a + b, terms)

    gm[...] = jnp.zeros(gm.shape, F32)
    gram_one = all_reduce(0, sums)
    low_one, inv_one = cholesky(gram_one, 5)
    linv_one = lower_inverse(low_one, inv_one, 5)
    half = {(i, j): add_up([linv_one[i, m] * gram_one(m, j) for m in range(i + 1)])
            for i in range(5) for j in range(i + 1)}
    gram_two = {(i, j): add_up([half[i, m] * linv_one[j, m] for m in range(j + 1)])
                for i in range(5) for j in range(i + 1)}
    low_two, inv_two = cholesky(lambda i, j: gram_two[i, j], 5)
    linv_two = lower_inverse(low_two, inv_two, 5)

    trans = {(i, j): add_up([linv_two[i, m] * linv_one[m, j] for m in range(j, i + 1)])
             for i in range(5) for j in range(i + 1)}
    rfac = {(i, j): add_up([low_two[m, i] * low_one[j, m] for m in range(i, j + 1)])
            for i in range(5) for j in range(i, 5)}
    shifted = {}
    for k in range(4):
        for i in range(k + 2):
            val = rfac[i, k + 1] * SCALE
            shifted[i, k] = val + rfac[i, k] * NEWTON[k] if i <= k else val
    hess = {(i, k): add_up([shifted[i, m] * trans[k, m] for m in range(max(i - 1, 0), k + 1)])
            for k in range(4) for i in range(k + 2)}
    target, inv_n = [rfac[0, 0]], []
    for k in range(4):
        top, bottom = hess[k, k], hess[k + 1, k]
        square = top * top + bottom * bottom
        inv_n.append(inv_sqrt(square))
        cosine, sine = top * inv_n[k], bottom * inv_n[k]
        for j in range(k + 1, 4):
            upper, under = hess[k, j], hess[k + 1, j]
            hess[k, j] = cosine * upper + sine * under
            hess[k + 1, j] = cosine * under - sine * upper
        target.append(-(sine * target[k]))
        target[k] = cosine * target[k]
    weights = [None] * 4
    for i in range(3, -1, -1):
        val = target[i]
        for m in range(i + 1, 4):
            val = val - hess[i, m] * weights[m]
        weights[i] = val * inv_n[i]

    root = math.sqrt(nrows * ncols * nx * ny * nz)
    for e, (j, i) in enumerate(PAIRS):
        coef_out[e:e + 1, :] = trans[i, j] * root
    for k in range(4):
        coef_out[16 + k:17 + k, :] = weights[k] * (1.0 / root)
    one_row = lax.broadcasted_iota(jnp.int32, (1, LANES), 1)
    for i in range(5):
        line = jnp.zeros((1, LANES), F32)
        column = [rfac[i, 0] if i == 0 else jnp.zeros((1, LANES), F32)]
        for j in range(1, 5):
            below = rfac[i, j] if j >= i else 0.0
            column.append(below - column[j - 1] * (SHIFTS[j - 1] / SCALE))
        for j in range(i, 5):
            line = jnp.where(one_row == j, column[j], line)
        coef_out[24 + i:25 + i, :] = line

    for cp in outs:
        cp.wait()
    for has_target, _, copy in sent:
        if has_target is None:
            copy.wait_send()
        else:
            @pl.when(has_target)
            def _(copy=copy):
                copy.wait_send()


def finish_kernel(v_ref, coef_ref, basis_ref, rfac_ref, updated_ref):
    _, rows, nz = v_ref.shape
    trans = {(i, j): jnp.broadcast_to(coef_ref[e:e + 1, :], (8, LANES))
             for e, (j, i) in enumerate(PAIRS)}
    weights = [jnp.broadcast_to(coef_ref[16 + k:17 + k, :], (8, LANES)) for k in range(4)]

    def body(n, carry):
        at = pl.ds(pl.multiple_of(n * 8, 8), 8)
        for h in range(nz // LANES):
            lanes = pl.ds(h * LANES, LANES)
            raw = [v_ref[k, at, lanes] for k in range(5)]
            new = v_ref[5, at, lanes]
            for i in range(5):
                val = trans[i, 0] * raw[0]
                for j in range(1, i + 1):
                    val = val + trans[i, j] * raw[j]
                basis_ref[i, at, lanes] = val
                if i < 4:
                    new = new + weights[i] * val
            updated_ref[at, lanes] = new
        return carry
    lax.fori_loop(0, rows // 8, body, 0, unroll=4)
    rfac_ref[...] = coef_ref[24:29, 0:5]


def on_device(nrows, ncols, right_side, initial, conduct):
    nx, ny, nz = initial.shape
    nh, count = nz // LANES, nx * ny
    flat = [a.reshape(count, nz) for a in (right_side, initial, conduct)]
    dma = pltpu.SemaphoreType.DMA
    slots = nrows * ncols
    vec = pltpu.VMEM((nh, count + ny, LANES), F32)
    plain = pltpu.VMEM((nh, count, LANES), F32)
    vectors, coefs = pl.pallas_call(
        functools.partial(cycle_kernel, (nrows, ncols, nx, ny, nz)),
        out_shape=(pltpu.VMEM((6, count, nz), F32),
                   pltpu.VMEM((32, LANES), F32)),
        in_specs=[pl.BlockSpec(memory_space=pltpu.HBM)] * 3,
        out_specs=(pl.BlockSpec(memory_space=pl.ANY), pl.BlockSpec(memory_space=pltpu.VMEM)),
        scratch_shapes=[
            pltpu.VMEM((2, nh, count + ny, LANES), F32), plain, vec, vec, vec, vec, plain,
            plain, plain, plain, plain, plain,
            pltpu.VMEM((2, nh, ny, LANES), F32), pltpu.VMEM((2, nh, nx, LANES), F32),
            pltpu.VMEM((6, 2, nh, nx, LANES), F32),
            pltpu.VMEM((6, 2, nh, ny, LANES), F32), pltpu.VMEM((6, 2, nh, nx, LANES), F32),
            pltpu.VMEM((1, slots, 1, LANES), F32), pltpu.VMEM((1, nrows, 1, LANES), F32),
            pltpu.VMEM((16, LANES), F32),
            dma((3, nh)), dma((6, nh)), dma((6, 4)), dma((6, 4)),
            dma((1, slots)), dma((1, slots)), dma((1, nrows)), dma((1, nrows)),
        ],
        compiler_params=pltpu.CompilerParams(
            collective_id=0, has_side_effects=True, vmem_limit_bytes=56 << 20),
        name="cycle",
    )(*flat)
    block = 256
    basis, rfactor, updated = pl.pallas_call(
        finish_kernel,
        grid=(count // block,),
        out_shape=(jax.ShapeDtypeStruct((5, count, nz), F32),
                   jax.ShapeDtypeStruct((5, 5), F32),
                   jax.ShapeDtypeStruct((count, nz), F32)),
        in_specs=[pl.BlockSpec((6, block, nz), lambda i: (0, i, 0)),
                  pl.BlockSpec((32, LANES), lambda i: (0, 0))],
        out_specs=(pl.BlockSpec((5, block, nz), lambda i: (0, i, 0)),
                   pl.BlockSpec((5, 5), lambda i: (0, 0)),
                   pl.BlockSpec((block, nz), lambda i: (i, 0))),
        compiler_params=pltpu.CompilerParams(vmem_limit_bytes=20 << 20),
        name="finish",
    )(vectors, coefs)
    return (basis.reshape(5, nx, ny, nz), rfactor, updated.reshape(nx, ny, nz))


def solution(mesh):
    nrows, ncols = mesh.shape["rows"], mesh.shape["cols"]
    return jax.shard_map(
        functools.partial(on_device, nrows, ncols),
        mesh=mesh,
        in_specs=(P("rows", "cols", None),) * 3,
        out_specs=(P(None, "rows", "cols", None), P(), P("rows", "cols", None)),
        check_vma=False,
    )
```

```python
import functools
import math

import jax
import jax.numpy as jnp
from jax import lax
from jax.experimental import pallas as pl
from jax.experimental.pallas import tpu as pltpu
from jax.sharding import PartitionSpec as P

SHIFTS = (12.0, 3.0, 21.0, 7.0)
NEWTON = (0.0,) + SHIFTS[:3]
SCALE = 8.0
LANES = 128
SUBS = 8
PLANES = 8
MESH = pl.DeviceIdType.MESH
PAIRS = [(i, j) for j in range(5) for i in range(j + 1)]
SUMS = [(0, 0)] + [(k - d, k) for k in range(1, 5) for d in (1, 0)]
F32 = jnp.float32


def inv_sqrt(value):
    guess = lax.rsqrt(value)
    return guess * (1.5 - 0.5 * (value * guess) * guess)


def cholesky(entry, order):
    lower, inv = {}, []
    for col in range(order):
        diag = entry(col, col)
        for inner in range(col):
            diag = diag - lower[col, inner] * lower[col, inner]
        root = inv_sqrt(diag)
        inv.append(root)
        lower[col, col] = diag * root
        for row in range(col + 1, order):
            val = entry(row, col)
            for inner in range(col):
                val = val - lower[row, inner] * lower[col, inner]
            lower[row, col] = val * root
    return lower, inv


def lower_inverse(lower, inv, order):
    result = {}
    for row in range(order):
        for col in range(row):
            total = lower[row, col] * result[col, col]
            for inner in range(col + 1, row):
                total = total + lower[row, inner] * result[inner, col]
            result[row, col] = -(total * inv[row])
        result[row, row] = inv[row]
    return result


def add_up(terms):
    return functools.reduce(lambda a, b: a + b, terms)


def cycle_kernel(sizes, rs_hbm, init_hbm, cond_hbm, w_out, coef_out,
                 kk, rs, diag, cx, cy, cyb, cz, czb, cfx, cfy, fy, hx, hy,
                 g1, g2, gm, load_sem, hs_sem, hr_sem, s1, r1, s2, r2, in_sem):
    nrows, ncols, nx, ny, nz = sizes
    nh, ng = nz // LANES, ny // SUBS
    count = nx * ny
    one_stage = nrows * ncols <= 64
    cells = [(h, g) for h in range(nh) for g in range(ng)]
    me_r, me_c = lax.axis_index("rows"), lax.axis_index("cols")
    uu = w_out.at[5]

    loads = []
    for idx, (src, dst) in enumerate(((cond_hbm, kk), (init_hbm, uu), (rs_hbm, rs))):
        for h in range(nh):
            loads.append(pltpu.make_async_copy(
                src.at[:, pl.ds(h * LANES, LANES)], dst.at[h, pl.ds(0, count), :],
                load_sem.at[idx, h]))
            loads[-1].start()

    barrier = pltpu.get_barrier_semaphore()
    col_peers = [(0, d) for d in range(1, ncols)]
    row_peers = [(d, 0) for d in range(1, nrows)]

    def device(dr, dc):
        return (lax.rem(me_r + dr, nrows), lax.rem(me_c + dc, ncols))

    for dr, dc in col_peers + row_peers:
        pl.semaphore_signal(barrier, inc=1, device_id_type=MESH, device_id=device(dr, dc))

    zero_plane = jnp.zeros((nh, ny, LANES), F32)
    kk[:, pl.ds(count, ny), :] = zero_plane
    for i in range(6):
        w_out[i, :, pl.ds(count, ny), :] = zero_plane
    for edge, ref, side in ((me_c == 0, hy, 0), (me_c == ncols - 1, hy, 1),
                            (me_r == 0, hx, 0), (me_r == nrows - 1, hx, 1)):
        @pl.when(edge)
        def _(ref=ref, side=side):
            for k in range(6):
                ref[k, side] = jnp.zeros(ref.shape[2:], F32)

    def strided(side):
        return pl.ds(0 if side == 0 else ny - 1, nx, stride=ny)

    def plane_at(side):
        return pl.ds(0 if side == 0 else count - ny, ny)

    sent = []

    def face_copies(k, vec):
        made = []
        for slot, axis, me, size in ((0, "cols", me_c, ncols), (1, "cols", me_c, ncols),
                                     (2, "rows", me_r, nrows), (3, "rows", me_r, nrows)):
            side = slot % 2
            target = me + 1 if side == 0 else me - 1
            has_target = me < size - 1 if side == 0 else me > 0
            has_source = me > 0 if side == 0 else me < size - 1
            if axis == "cols":
                src, dst = fy.at[k, 1 - side], hy.at[k, side]
            else:
                src, dst = vec.at[:, plane_at(1 - side), :], hx.at[k, side]
            made.append((has_target, has_source, pltpu.make_async_remote_copy(
                src_ref=src, dst_ref=dst, send_sem=hs_sem.at[k, slot],
                recv_sem=hr_sem.at[k, slot], device_id={axis: target}, device_id_type=MESH)))
        return made

    def send(copies):
        sent.extend(copies)
        for has_target, _, copy in copies:
            @pl.when(has_target)
            def _(copy=copy):
                copy.start()

    def arrive(copies):
        for _, has_source, copy in copies:
            @pl.when(has_source)
            def _(copy=copy):
                copy.wait_recv()

    first = []
    for i, ref in enumerate((kk, uu)):
        for cp in loads[i * nh:(i + 1) * nh]:
            cp.wait()
        for side in range(2):
            for h in range(nh):
                fy[i, side, h] = ref[h, strided(side), :]
        first += face_copies(i, ref)
    pl.semaphore_wait(barrier, len(col_peers) + len(row_peers))
    send(first)
    if one_stage:
        for dr, dc in row_peers:
            pl.semaphore_signal(in_sem, inc=1, device_id_type=MESH, device_id=device(dr, dc))

    lane = lax.broadcasted_iota(jnp.int32, (SUBS, LANES), 1)
    sub = lax.broadcasted_iota(jnp.int32, (SUBS, LANES), 0)
    first_lane, last_lane = lane == 0, lane == LANES - 1
    first_sub, last_sub = sub == 0, sub == SUBS - 1
    zero = jnp.zeros((SUBS, LANES), F32)
    sixteenth = 0.5 / SCALE

    def tile(ref, h, g, base):
        return ref[h, pl.ds(base + g * SUBS, SUBS), :]

    def get(ref, base):
        return {(h, g): tile(ref, h, g, base) for h, g in cells}

    def put(ref, base, values):
        for h, g in cells:
            ref[h, pl.ds(base + g * SUBS, SUBS), :] = values[h, g]

    def y_up(v):
        r = {c: pltpu.roll(v[c], SUBS - 1, 0) for c in cells}
        return {(h, g): jnp.where(last_sub, r[h, g + 1], r[h, g]) if g < ng - 1 else r[h, g]
                for h, g in cells}

    def y_down(v):
        r = {c: pltpu.roll(v[c], 1, 0) for c in cells}
        return {(h, g): jnp.where(first_sub, r[h, g - 1], r[h, g]) if g > 0 else r[h, g]
                for h, g in cells}

    def z_up(v):
        r = {c: pltpu.roll(v[c], LANES - 1, 1) for c in cells}
        return {(h, g): jnp.where(last_lane, r[h + 1, g], r[h, g]) if h < nh - 1 else r[h, g]
                for h, g in cells}

    def z_down(v):
        r = {c: pltpu.roll(v[c], 1, 1) for c in cells}
        return {(h, g): jnp.where(first_lane, r[h - 1, g], r[h, g]) if h > 0 else r[h, g]
                for h, g in cells}

    flat = lambda v: tuple(v[c] for c in cells)
    dict_of = lambda t: dict(zip(cells, t))

    def coef_body(i, carry):
        here, cx_before = dict_of(carry[0]), dict_of(carry[1])
        for q in range(PLANES):
            base = pl.multiple_of((i * PLANES + q) * ny, ny)
            after = get(kk, base + ny)
            up, right = y_up(here), z_up(here)
            fx = {c: (here[c] + after[c]) * sixteenth for c in cells}
            fy_ = {c: (here[c] + up[c]) * sixteenth for c in cells}
            fz = {c: (here[c] + right[c]) * sixteenth for c in cells}
            for h in range(nh):
                fy_[h, ng - 1] = jnp.where(last_sub, 0.0, fy_[h, ng - 1])
            for g in range(ng):
                fz[nh - 1, g] = jnp.where(last_lane, 0.0, fz[nh - 1, g])
            fyb, fzb = y_down(fy_), z_down(fz)
            for h in range(nh):
                fyb[h, 0] = jnp.where(first_sub, 0.0, fyb[h, 0])
            for g in range(ng):
                fzb[0, g] = jnp.where(first_lane, 0.0, fzb[0, g])
            total = {c: ((fx[c] + cx_before[c]) + (fy_[c] + fyb[c])) + (fz[c] + fzb[c])
                     for c in cells}
            for g in range(ng):
                total[0, g] = total[0, g] + jnp.where(first_lane, here[0, g] * sixteenth, 0.0)
                total[nh - 1, g] = total[nh - 1, g] + jnp.where(
                    last_lane, here[nh - 1, g] * sixteenth, 0.0)
            put(cx, base, fx)
            put(cy, base, fy_)
            put(cyb, base, fyb)
            put(cz, base, fz)
            put(czb, base, fzb)
            put(diag, base, total)
            here, cx_before = after, fx
        return flat(here), flat(cx_before)

    lax.fori_loop(0, nx // PLANES, coef_body, (flat(get(kk, 0)), (zero,) * len(cells)))
    last = count - ny
    put(diag, last, {c: tile(diag, *c, last) - tile(cx, *c, last) for c in cells})
    put(cx, last, {c: zero for c in cells})

    def stencil(src, dst, shift, residual, pairs):
        def body(i, carry):
            here, before, cx_before = (dict_of(t) for t in carry[:3])
            accs = [dict_of(t) for t in carry[3]]
            for q in range(PLANES):
                base = pl.multiple_of((i * PLANES + q) * ny, ny)
                after = get(src, base + ny)
                up, down, right, left = y_up(here), y_down(here), z_up(here), z_down(here)
                new = {}
                fx = get(cx, base)
                for c in cells:
                    d = tile(diag, *c, base)
                    val = (d - shift if shift else d) * here[c]
                    val = val - fx[c] * after[c]
                    val = val - cx_before[c] * before[c]
                    val = val - tile(cy, *c, base) * up[c]
                    val = val - tile(cyb, *c, base) * down[c]
                    val = val - tile(cz, *c, base) * right[c]
                    val = val - tile(czb, *c, base) * left[c]
                    if residual:
                        val = tile(rs, *c, base) - SCALE * val
                    new[c] = val
                    for acc, other in zip(accs, pairs):
                        mate = here[c] if other is None else tile(other, *c, base)
                        acc[c] = acc[c] + here[c] * mate
                put(dst, base, new)
                before, here, cx_before = here, after, fx
            return flat(here), flat(before), flat(cx_before), tuple(flat(a) for a in accs)
        nothing = (zero,) * len(cells)
        out = lax.fori_loop(0, nx // PLANES, body,
                            (flat(get(src, 0)), nothing, nothing, (nothing,) * len(pairs)))
        return [add_up(list(t)) for t in out[3]]

    def corrections(k, src, dst, sign, pack):
        for side in range(2):
            at = plane_at(side)
            dst[:, at, :] = dst[:, at, :] + sign * (cfx[side] * (src[:, at, :] - hx[k, side]))
        for side in range(2):
            for h in range(nh):
                new = dst[h, strided(side), :] + sign * (
                    cfy[side, h] * (fy[k, side, h] - hy[k, side, h]))
                dst[h, strided(side), :] = new
                if pack:
                    fy[k + 1, side, h] = new

    for cp in loads[2 * nh:]:
        cp.wait()
    w = [w_out.at[k] for k in range(5)]
    stencil(uu, w[0], 0.0, True, [])
    arrive(first)
    for side in range(2):
        at = plane_at(side)
        cfx[side] = (kk[:, at, :] + hx[0, side]) * sixteenth
        cfy[side] = (fy[0, side] + hy[0, side]) * sixteenth
    corrections(1, uu, w[0], -SCALE, True)

    sums = {}
    for k in range(4):
        copies = face_copies(2 + k, w[k])
        send(copies)
        mates = [None] if k == 0 else [None, w[k - 1]]
        made = stencil(w[k], w[k + 1], NEWTON[k] / SCALE, False, mates)
        sums[k, k] = made[0]
        if k:
            sums[k - 1, k] = made[1]
        arrive(copies)
        corrections(2 + k, w[k], w[k + 1], 1.0, k < 3)

    def tail(i, carry):
        accs = [list(t) for t in carry]
        for q in range(PLANES):
            base = pl.multiple_of((i * PLANES + q) * ny, ny)
            for e, c in enumerate(cells):
                mine = tile(w[4], *c, base)
                accs[0][e] = accs[0][e] + mine * mine
                accs[1][e] = accs[1][e] + mine * tile(w[3], *c, base)
        return tuple(tuple(a) for a in accs)
    made = lax.fori_loop(0, nx // PLANES, tail, ((zero,) * len(cells),) * 2)
    sums[4, 4], sums[3, 4] = (add_up(list(t)) for t in made)

    def exchange(buf, ssem, rsem, peers, value):
        here = len(peers)
        buf[here] = value
        for e, (dr, dc) in enumerate(peers):
            pltpu.make_async_remote_copy(
                src_ref=buf.at[here], dst_ref=buf.at[e], send_sem=ssem.at[0], recv_sem=rsem.at[0],
                device_id=device(dr, dc), device_id_type=MESH).start()
        whole = buf.at[pl.ds(0, here)]
        pltpu.make_async_copy(whole, whole, rsem.at[0]).wait()
        parts = [buf[i] for i in range(here + 1)]
        while len(parts) > 1:
            parts = [a + b for a, b in zip(parts[::2], parts[1::2])] + (
                parts[-1:] if len(parts) % 2 else [])
        return parts[0]

    def finish_sends(buf, ssem, peers):
        whole = buf.at[pl.ds(0, len(peers))]
        pltpu.make_async_copy(whole, whole, ssem.at[0]).wait()

    everyone = [(dr, dc) for dr in range(nrows) for dc in range(ncols)][1:]
    pair_row = lax.broadcasted_iota(jnp.int32, (16, LANES), 0)
    on_diag = pair_row == lax.broadcasted_iota(jnp.int32, (16, LANES), 1)
    gm[...] = jnp.zeros(gm.shape, F32)
    for e, pair in enumerate(SUMS):
        gm[e:e + 1, :] = jnp.sum(sums[pair], axis=0, keepdims=True)
    line = jnp.sum(jnp.where(on_diag, jnp.sum(gm[...], axis=1, keepdims=True), 0.0),
                   axis=0, keepdims=True)
    if one_stage:
        pl.semaphore_wait(in_sem, len(row_peers))
        line = exchange(g1, s1, r1, everyone, line)
    else:
        line = exchange(g1, s1, r1, col_peers, line)
        line = exchange(g2, s2, r2, row_peers, line)
    gm[...] = jnp.broadcast_to(
        jnp.sum(jnp.where(on_diag, line, 0.0), axis=1, keepdims=True), gm.shape)
    moments = {pair: gm[e:e + 1, :] for e, pair in enumerate(SUMS)}
    for gap in range(2, 5):
        for i in range(5 - gap):
            j = i + gap
            moments[i, j] = moments[i + 1, j - 1] + (
                (NEWTON[i] - NEWTON[j - 1]) / SCALE) * moments[i, j - 1]
            moments[i, j] = moments[i, j]
    gram_one = lambda i, j: moments[min(i, j), max(i, j)]
    low_one, inv_one = cholesky(gram_one, 5)
    linv_one = lower_inverse(low_one, inv_one, 5)
    half = {(i, j): add_up([linv_one[i, m] * gram_one(m, j) for m in range(i + 1)])
            for i in range(5) for j in range(i + 1)}
    gram_two = {(i, j): add_up([half[i, m] * linv_one[j, m] for m in range(j + 1)])
                for i in range(5) for j in range(i + 1)}
    low_two, inv_two = cholesky(lambda i, j: gram_two[i, j], 5)
    linv_two = lower_inverse(low_two, inv_two, 5)

    trans = {(i, j): add_up([linv_two[i, m] * linv_one[m, j] for m in range(j, i + 1)])
             for i in range(5) for j in range(i + 1)}
    rfac = {(i, j): add_up([low_two[m, i] * low_one[j, m] for m in range(i, j + 1)])
            for i in range(5) for j in range(i, 5)}
    shifted = {}
    for k in range(4):
        for i in range(k + 2):
            val = rfac[i, k + 1] * SCALE
            shifted[i, k] = val + rfac[i, k] * NEWTON[k] if i <= k else val
    hess = {(i, k): add_up([shifted[i, m] * trans[k, m] for m in range(max(i - 1, 0), k + 1)])
            for k in range(4) for i in range(k + 2)}
    target, inv_n = [rfac[0, 0]], []
    for k in range(4):
        top, bottom = hess[k, k], hess[k + 1, k]
        square = top * top + bottom * bottom
        inv_n.append(inv_sqrt(square))
        cosine, sine = top * inv_n[k], bottom * inv_n[k]
        for j in range(k + 1, 4):
            upper, under = hess[k, j], hess[k + 1, j]
            hess[k, j] = cosine * upper + sine * under
            hess[k + 1, j] = cosine * under - sine * upper
        target.append(-(sine * target[k]))
        target[k] = cosine * target[k]
    weights = [None] * 4
    for i in range(3, -1, -1):
        val = target[i]
        for m in range(i + 1, 4):
            val = val - hess[i, m] * weights[m]
        weights[i] = val * inv_n[i]

    root = math.sqrt(nrows * ncols * nx * ny * nz)
    for e, (j, i) in enumerate(PAIRS):
        coef_out[e:e + 1, :] = trans[i, j] * root
    for k in range(4):
        coef_out[16 + k:17 + k, :] = weights[k] * (1.0 / root)
    one_row = lax.broadcasted_iota(jnp.int32, (1, LANES), 1)
    for i in range(5):
        line = jnp.zeros((1, LANES), F32)
        column = [rfac[i, 0] if i == 0 else jnp.zeros((1, LANES), F32)]
        for j in range(1, 5):
            below = rfac[i, j] if j >= i else 0.0
            column.append(below - column[j - 1] * (SHIFTS[j - 1] / SCALE))
        for j in range(i, 5):
            line = jnp.where(one_row == j, column[j], line)
        coef_out[24 + i:25 + i, :] = line

    if one_stage:
        finish_sends(g1, s1, everyone)
    else:
        finish_sends(g1, s1, col_peers)
        finish_sends(g2, s2, row_peers)
    for has_target, _, copy in sent:
        @pl.when(has_target)
        def _(copy=copy):
            copy.wait_send()


def finish_kernel(sizes, w_ref, coef_ref, basis_hbm, rfac_ref, updated_hbm, stage, sems):
    count, nz, chunk = sizes
    trans = {(i, j): jnp.broadcast_to(coef_ref[e:e + 1, :], (SUBS, LANES))
             for e, (j, i) in enumerate(PAIRS)}
    weights = [jnp.broadcast_to(coef_ref[16 + k:17 + k, :], (SUBS, LANES)) for k in range(4)]
    rfac_ref[...] = coef_ref[24:29, 0:5]
    copies = []
    for part in range(count // chunk):
        start = part * chunk

        def body(n, carry):
            at = pl.ds(pl.multiple_of(start + n * SUBS, SUBS), SUBS)
            for h in range(nz // LANES):
                lanes = pl.ds(h * LANES, LANES)
                raw = [w_ref[k, h, at, :] for k in range(5)]
                new = w_ref[5, h, at, :]
                for i in range(5):
                    val = trans[i, 0] * raw[0]
                    for j in range(1, i + 1):
                        val = val + trans[i, j] * raw[j]
                    stage[i, at, lanes] = val
                    if i < 4:
                        new = new + weights[i] * val
                stage[5, at, lanes] = new
            return carry
        lax.fori_loop(0, chunk // SUBS, body, 0, unroll=2)
        rows = pl.ds(start, chunk)
        for i in range(6):
            dst = basis_hbm.at[i, rows, :] if i < 5 else updated_hbm.at[rows, :]
            copies.append(pltpu.make_async_copy(stage.at[i, rows, :], dst, sems.at[part, i]))
            copies[-1].start()
    for copy in copies:
        copy.wait()


def on_device(nrows, ncols, right_side, initial, conduct):
    nx, ny, nz = initial.shape
    nh, count = nz // LANES, nx * ny
    flat = [a.reshape(count, nz) for a in (right_side, initial, conduct)]
    dma = pltpu.SemaphoreType.DMA
    slots = nrows * ncols if nrows * ncols <= 64 else ncols
    field = pltpu.VMEM((nh, count, LANES), F32)
    vectors, coefs = pl.pallas_call(
        functools.partial(cycle_kernel, (nrows, ncols, nx, ny, nz)),
        out_shape=(pltpu.VMEM((6, nh, count + ny, LANES), F32),
                   pltpu.VMEM((32, LANES), F32)),
        in_specs=[pl.BlockSpec(memory_space=pltpu.HBM)] * 3,
        out_specs=(pl.BlockSpec(memory_space=pltpu.VMEM), pl.BlockSpec(memory_space=pltpu.VMEM)),
        scratch_shapes=[
            pltpu.VMEM((nh, count + ny, LANES), F32),
            field, field, field, field, field, field, field,
            pltpu.VMEM((2, nh, ny, LANES), F32), pltpu.VMEM((2, nh, nx, LANES), F32),
            pltpu.VMEM((6, 2, nh, nx, LANES), F32),
            pltpu.VMEM((6, 2, nh, ny, LANES), F32), pltpu.VMEM((6, 2, nh, nx, LANES), F32),
            pltpu.VMEM((slots, 1, LANES), F32), pltpu.VMEM((nrows, 1, LANES), F32),
            pltpu.VMEM((16, LANES), F32),
            dma((3, nh)), dma((6, 4)), dma((6, 4)),
            dma((1,)), dma((1,)), dma((1,)), dma((1,)), pltpu.SemaphoreType.REGULAR,
        ],
        compiler_params=pltpu.CompilerParams(
            collective_id=0, has_side_effects=True, vmem_limit_bytes=57 << 20),
        name="cycle",
    )(*flat)
    chunk = min(128, count)
    basis, rfactor, updated = pl.pallas_call(
        functools.partial(finish_kernel, (count, nz, chunk)),
        out_shape=(jax.ShapeDtypeStruct((5, count, nz), F32),
                   jax.ShapeDtypeStruct((5, 5), F32),
                   jax.ShapeDtypeStruct((count, nz), F32)),
        in_specs=[pl.BlockSpec(memory_space=pltpu.VMEM)] * 2,
        out_specs=(pl.BlockSpec(memory_space=pltpu.HBM), pl.BlockSpec(memory_space=pltpu.VMEM),
                   pl.BlockSpec(memory_space=pltpu.HBM)),
        scratch_shapes=[pltpu.VMEM((6, count, nz), F32), dma((count // chunk, 6))],
        compiler_params=pltpu.CompilerParams(vmem_limit_bytes=20 << 20),
        name="finish",
    )(vectors, coefs)
    return (basis.reshape(5, nx, ny, nz), rfactor, updated.reshape(nx, ny, nz))


def solution(mesh):
    nrows, ncols = mesh.shape["rows"], mesh.shape["cols"]
    return jax.shard_map(
        functools.partial(on_device, nrows, ncols),
        mesh=mesh,
        in_specs=(P("rows", "cols", None),) * 3,
        out_specs=(P(None, "rows", "cols", None), P(), P("rows", "cols", None)),
        check_vma=False,
    )
```

```python
import functools
import math

import jax
import jax.numpy as jnp
from jax import lax
from jax.experimental import pallas as pl
from jax.experimental.pallas import tpu as pltpu
from jax.sharding import PartitionSpec as P

SHIFTS = (12.0, 3.0, 21.0, 7.0)
NEWTON = (0.0,) + SHIFTS[:3]
SCALE = 8.0
LANES = 128
SUBS = 8
PLANES = 8
OFF = SUBS
MESH = pl.DeviceIdType.MESH
PAIRS = [(i, j) for j in range(5) for i in range(j + 1)]
SUMS = [(0, 0)] + [(k - d, k) for k in range(1, 5) for d in (1, 0)]
F32 = jnp.float32


def inv_sqrt(value):
    guess = lax.rsqrt(value)
    return guess * (1.5 - 0.5 * (value * guess) * guess)


def cholesky(entry, order):
    lower, inv = {}, []
    for col in range(order):
        diag = entry(col, col)
        for inner in range(col):
            diag = diag - lower[col, inner] * lower[col, inner]
        root = inv_sqrt(diag)
        inv.append(root)
        lower[col, col] = diag * root
        for row in range(col + 1, order):
            val = entry(row, col)
            for inner in range(col):
                val = val - lower[row, inner] * lower[col, inner]
            lower[row, col] = val * root
    return lower, inv


def lower_inverse(lower, inv, order):
    result = {}
    for row in range(order):
        for col in range(row):
            total = lower[row, col] * result[col, col]
            for inner in range(col + 1, row):
                total = total + lower[row, inner] * result[inner, col]
            result[row, col] = -(total * inv[row])
        result[row, row] = inv[row]
    return result


def add_up(terms):
    return functools.reduce(lambda a, b: a + b, terms)


def cycle_kernel(sizes, rs_hbm, init_hbm, cond_hbm, w_out, coef_out,
                 kk, rs, diag, cx, cy, cyb, cz, czb, cfx, cfy,
                 fyk, fyu, fyw, gyk, gyu, gyw, gxk, gxu, gxw, ck, cw, gck, gcw,
                 ghost_y, ghost_x, own_y, bump_y, bump_x,
                 g1, g2, gm, load_sem, hs_sem, hr_sem, s1, r1, s2, r2, in_sem):
    nrows, ncols, nx, ny, nz = sizes
    nh, ng = nz // LANES, ny // SUBS
    count = nx * ny
    one_stage = nrows * ncols <= 64
    halves = range(nh)
    cells = [(h, g) for h in halves for g in range(ng)]
    me_r, me_c = lax.axis_index("rows"), lax.axis_index("cols")
    uu = w_out.at[5]
    w = [w_out.at[k] for k in range(5)]
    inner = pl.ds(OFF, count)

    loads = []
    for idx, (src, dst) in enumerate(((cond_hbm, kk), (init_hbm, uu), (rs_hbm, rs))):
        for h in halves:
            loads.append(pltpu.make_async_copy(
                src.at[:, pl.ds(h * LANES, LANES)],
                dst.at[h, inner if idx < 2 else pl.ds(0, count), :], load_sem.at[idx, h]))
            loads[-1].start()

    barrier = pltpu.get_barrier_semaphore()
    col_peers = [(0, d) for d in range(1, ncols)]
    row_peers = [(d, 0) for d in range(1, nrows)]
    greeted = col_peers + row_peers + sorted(
        {(dr % nrows, dc % ncols) for dr in (-1, 1) for dc in (-1, 1)}
        - set(col_peers + row_peers + [(0, 0)]))

    def device(dr, dc):
        return (lax.rem(me_r + dr, nrows), lax.rem(me_c + dc, ncols))

    for dr, dc in greeted:
        pl.semaphore_signal(barrier, inc=1, device_id_type=MESH, device_id=device(dr, dc))

    for ref in [kk] + [w_out.at[i] for i in range(6)]:
        ref[:, pl.ds(0, OFF), :] = jnp.zeros((nh, OFF, LANES), F32)
        ref[:, pl.ds(OFF + count, ny), :] = jnp.zeros((nh, ny, LANES), F32)
    for ref, length in ((bump_y, nx), (bump_x, ny)):
        for row in (0, SUBS + length):
            ref[:, pl.ds(row, SUBS), :] = jnp.zeros((nh, SUBS, LANES), F32)
    edge_c, edge_r = (me_c == 0, me_c == ncols - 1), (me_r == 0, me_r == nrows - 1)
    for side in range(2):
        @pl.when(edge_c[side])
        def _(side=side):
            for ref in (gyk.at[side], gyu.at[side], gyw.at[0, side], gyw.at[1, side]):
                ref[...] = jnp.zeros(ref.shape, F32)

        @pl.when(edge_r[side])
        def _(side=side):
            for ref in (gxk.at[side], gxu.at[side], gxw.at[0, side], gxw.at[1, side]):
                ref[...] = jnp.zeros(ref.shape, F32)
        for other in range(2):
            @pl.when(jnp.logical_or(edge_r[side], edge_c[other]))
            def _(q=2 * side + other):
                for ref in (gck.at[q], gcw.at[0, q], gcw.at[1, q]):
                    ref[...] = jnp.zeros(ref.shape, F32)

    sent = []

    def transfer(src, dst, dr, dc):
        def exists(step_r, step_c):
            tests = []
            if step_r:
                tests.append(me_r < nrows - 1 if step_r > 0 else me_r > 0)
            if step_c:
                tests.append(me_c < ncols - 1 if step_c > 0 else me_c > 0)
            return functools.reduce(jnp.logical_and, tests)
        n = len(sent)
        copy = pltpu.make_async_remote_copy(
            src_ref=src, dst_ref=dst, send_sem=hs_sem.at[n], recv_sem=hr_sem.at[n],
            device_id=(me_r + dr, me_c + dc), device_id_type=MESH)
        has_target = exists(dr, dc)
        sent.append((has_target, copy))

        @pl.when(has_target)
        def _():
            copy.start()
        return exists(-dr, -dc), copy

    def arrive(copies):
        for has_source, copy in copies:
            @pl.when(has_source)
            def _(copy=copy):
                copy.wait_recv()

    def toward(side):
        return 1 if side == 0 else -1

    def strided(side, depth=0):
        return pl.ds(OFF + (depth if side == 0 else ny - 1 - depth), nx, stride=ny)

    def plane_at(side, depth=0):
        return pl.ds(OFF + (depth if side == 0 else nx - 1 - depth) * ny, ny)

    def corner_at(q):
        return pl.ds(OFF + (q // 2) * (nx - 1) * ny + (q % 2) * (ny - 1), 1)

    along = pl.ds(SUBS, nx)
    across = pl.ds(SUBS, ny)

    def send_corners(ref, mine, theirs):
        made = []
        for q in range(4):
            mine[q] = ref[:, corner_at(q), :]
        for q in range(4):
            made.append(transfer(mine.at[3 - q], theirs.at[q], toward(q // 2), toward(q % 2)))
        return made

    for cp in loads[:2 * nh]:
        cp.wait()
    for side in range(2):
        for h in halves:
            fyk[side, 0, h] = kk[h, strided(side), :]
            fyu[side, h] = uu[h, strided(side), :]
    pl.semaphore_wait(barrier, len(greeted))
    first, second = [], []
    for side in range(2):
        t = toward(side)
        first.append(transfer(fyk.at[1 - side, 0], gyk.at[side, 0, :, along, :], 0, t))
        first.append(transfer(fyu.at[1 - side], gyu.at[side], 0, t))
    for side in range(2):
        t = toward(side)
        first.append(transfer(kk.at[:, plane_at(1 - side), :], gxk.at[side, 0, :, across, :], t, 0))
        first.append(transfer(uu.at[:, plane_at(1 - side), :], gxu.at[side], t, 0))
    for side in range(2):
        for h in halves:
            fyk[side, 1, h] = kk[h, strided(side, 1), :]
    for side in range(2):
        t = toward(side)
        second.append(transfer(fyk.at[1 - side, 1], gyk.at[side, 1, :, along, :], 0, t))
        second.append(transfer(kk.at[:, plane_at(1 - side, 1), :], gxk.at[side, 1, :, across, :], t, 0))
    second += send_corners(kk, ck, gck)
    if one_stage:
        for dr, dc in row_peers:
            pl.semaphore_signal(in_sem, inc=1, device_id_type=MESH, device_id=device(dr, dc))

    lane = lax.broadcasted_iota(jnp.int32, (SUBS, LANES), 1)
    sub = lax.broadcasted_iota(jnp.int32, (SUBS, LANES), 0)
    first_lane, last_lane = lane == 0, lane == LANES - 1
    first_sub, last_sub = sub == 0, sub == SUBS - 1
    zero = jnp.zeros((SUBS, LANES), F32)
    sixteenth = 0.5 / SCALE

    def tile(ref, h, g, base, offset=0):
        return ref[h, pl.ds(base + (g * SUBS + offset), SUBS), :]

    def get(ref, base, offset=0):
        return {(h, g): tile(ref, h, g, base, offset) for h, g in cells}

    def put(ref, base, values):
        for h, g in cells:
            ref[h, pl.ds(base + g * SUBS, SUBS), :] = values[h, g]

    def y_down(v):
        r = {c: pltpu.roll(v[c], 1, 0) for c in cells}
        return {(h, g): jnp.where(first_sub, r[h, g - 1], r[h, g]) if g > 0 else r[h, g]
                for h, g in cells}

    def z_up(v):
        r = {c: pltpu.roll(v[c], LANES - 1, 1) for c in v}
        return {(h, g): jnp.where(last_lane, r[h + 1, g], r[h, g]) if h < nh - 1 else r[h, g]
                for h, g in v}

    def z_down(v):
        r = {c: pltpu.roll(v[c], 1, 1) for c in v}
        return {(h, g): jnp.where(first_lane, r[h - 1, g], r[h, g]) if h > 0 else r[h, g]
                for h, g in v}

    flat = lambda v: tuple(v[c] for c in cells)
    dict_of = lambda t: dict(zip(cells, t))

    def coef_body(i, carry):
        here, cx_before = dict_of(carry[0]), dict_of(carry[1])
        for q in range(PLANES):
            low = pl.multiple_of((i * PLANES + q) * ny, ny)
            base = low + OFF
            after = get(kk, base + ny)
            up, right = get(kk, base, 1), z_up(here)
            fx = {c: (here[c] + after[c]) * sixteenth for c in cells}
            fy_ = {c: (here[c] + up[c]) * sixteenth for c in cells}
            fz = {c: (here[c] + right[c]) * sixteenth for c in cells}
            for h in halves:
                fy_[h, ng - 1] = jnp.where(last_sub, 0.0, fy_[h, ng - 1])
            for g in range(ng):
                fz[nh - 1, g] = jnp.where(last_lane, 0.0, fz[nh - 1, g])
            fyb, fzb = y_down(fy_), z_down(fz)
            for h in halves:
                fyb[h, 0] = jnp.where(first_sub, 0.0, fyb[h, 0])
            for g in range(ng):
                fzb[0, g] = jnp.where(first_lane, 0.0, fzb[0, g])
            total = {c: ((fx[c] + cx_before[c]) + (fy_[c] + fyb[c])) + (fz[c] + fzb[c])
                     for c in cells}
            for g in range(ng):
                total[0, g] = total[0, g] + jnp.where(first_lane, here[0, g] * sixteenth, 0.0)
                total[nh - 1, g] = total[nh - 1, g] + jnp.where(
                    last_lane, here[nh - 1, g] * sixteenth, 0.0)
            for ref, val in ((cx, fx), (cy, fy_), (cyb, fyb), (cz, fz), (czb, fzb), (diag, total)):
                put(ref, base, val)
            here, cx_before = after, fx
        return flat(here), flat(cx_before)

    lax.fori_loop(0, nx // PLANES, coef_body, (flat(get(kk, OFF)), (zero,) * len(cells)))
    last = OFF + count - ny
    put(diag, last, {c: tile(diag, *c, last) - tile(cx, *c, last) for c in cells})
    put(cx, last, {c: zero for c in cells})

    def products(accs, pairs, here, base):
        for acc, (one, two) in zip(accs, pairs):
            for c in cells:
                left = here[c] if one is None else tile(one, *c, base)
                right = here[c] if two is None else tile(two, *c, base)
                acc[c] = acc[c] + left * right

    def stencil(src, dst, shift, residual, pairs):
        def body(i, carry):
            here, before, cx_before = (dict_of(t) for t in carry[:3])
            accs = [dict_of(t) for t in carry[3]]
            for q in range(PLANES):
                low = pl.multiple_of((i * PLANES + q) * ny, ny)
                base = low + OFF
                after = get(src, base + ny)
                up, down, right, left = get(src, base, 1), get(src, base, -1), z_up(here), z_down(here)
                new = {}
                fx = get(cx, base)
                for c in cells:
                    d = tile(diag, *c, base)
                    val = (d - shift if shift else d) * here[c]
                    val = val - fx[c] * after[c]
                    val = val - cx_before[c] * before[c]
                    val = val - tile(cy, *c, base) * up[c]
                    val = val - tile(cyb, *c, base) * down[c]
                    val = val - tile(cz, *c, base) * right[c]
                    val = val - tile(czb, *c, base) * left[c]
                    if residual:
                        val = tile(rs, *c, low) - SCALE * val
                    new[c] = val
                products(accs, pairs, here, base)
                put(dst, base, new)
                before, here, cx_before = here, after, fx
            return flat(here), flat(before), flat(cx_before), tuple(flat(a) for a in accs)
        nothing = (zero,) * len(cells)
        out = lax.fori_loop(0, nx // PLANES, body,
                            (flat(get(src, OFF)), nothing, nothing, (nothing,) * len(pairs)))
        return [add_up(list(t)) for t in out[3]]

    def grams(pairs):
        def body(i, carry):
            accs = [dict_of(t) for t in carry]
            for q in range(PLANES):
                low = pl.multiple_of((i * PLANES + q) * ny, ny)
                products(accs, pairs, None, low + OFF)
            return tuple(flat(a) for a in accs)
        out = lax.fori_loop(0, nx // PLANES, body, ((zero,) * len(cells),) * len(pairs))
        return [add_up(list(t)) for t in out]

    for cp in loads[2 * nh:]:
        cp.wait()
    stencil(uu, w[0], 0.0, True, [])
    arrive(first)
    for side in range(2):
        at = plane_at(side)
        coef = (kk[:, at, :] + gxk[side, 0, :, across, :]) * sixteenth
        cfx[side] = coef
        w[0][:, at, :] = w[0][:, at, :] - SCALE * (coef * (uu[:, at, :] - gxu[side]))
    for side in range(2):
        for h in halves:
            coef = (fyk[side, 0, h] + gyk[side, 0, h, along, :]) * sixteenth
            cfy[side, h] = coef
            new = w[0][h, strided(side), :] - SCALE * (coef * (fyu[side, h] - gyu[side, h]))
            w[0][h, strided(side), :] = new
            fyw[0, side, 0, h] = new
            fyw[0, side, 1, h] = w[0][h, strided(side, 1), :]

    def send_layers(r, ref):
        made = []
        for side in range(2):
            made.append(transfer(fyw.at[r, 1 - side], gyw.at[r, side, :, :, along, :], 0, toward(side)))
        for side in range(2):
            for depth in range(2):
                made.append(transfer(ref.at[:, plane_at(1 - side, depth), :],
                                     gxw.at[r, side, depth, :, across, :], toward(side), 0))
        return made + send_corners(ref, cw.at[r], gcw.at[r])

    def sideways(values, step):
        length = values[0].shape[0]
        index = lax.broadcasted_iota(jnp.int32, (length, LANES), 1)
        rolled = [pltpu.roll(v, LANES - 1 if step > 0 else 1, 1) for v in values]
        made = []
        for h in halves:
            if step > 0 and h < nh - 1:
                made.append(jnp.where(index == LANES - 1, rolled[h + 1], rolled[h]))
            elif step < 0 and h > 0:
                made.append(jnp.where(index == 0, rolled[h - 1], rolled[h]))
            else:
                made.append(rolled[h])
        return made

    def shifted_rows(ref, length, step):
        return [ref[h, pl.ds(SUBS + step, length), :] for h in halves]

    def corners_into(planes, low, high, length):
        planes[:, pl.ds(SUBS - 1, 1), :] = low[...]
        planes[:, pl.ds(SUBS + length, 1), :] = high[...]

    def corner_rows(gy, gx, theirs):
        for side in range(2):
            corners_into(gy[side], theirs.at[side], theirs.at[2 + side], nx)
            corners_into(gx[side], theirs.at[2 * side], theirs.at[2 * side + 1], ny)

    def ghost_coefs(near, far, face, length, out):
        here, up, down = (shifted_rows(near, length, s) for s in (0, 1, -1))
        beyond = shifted_rows(far, length, 0)
        right = sideways(here, 1)
        index = lax.broadcasted_iota(jnp.int32, (length, LANES), 1)
        fz = [(here[h] + right[h]) * sixteenth for h in halves]
        fz[-1] = jnp.where(index == LANES - 1, 0.0, fz[-1])
        fzb = sideways(fz, -1)
        fzb[0] = jnp.where(index == 0, 0.0, fzb[0])
        for h in halves:
            fu, fd, fn = ((here[h] + v[h]) * sixteenth for v in (up, down, beyond))
            total = ((fu + fd) + (fn + face[h])) + (fz[h] + fzb[h])
            if h == 0:
                total = total + jnp.where(index == 0, here[h] * sixteenth, 0.0)
            if h == nh - 1:
                total = total + jnp.where(index == LANES - 1, here[h] * sixteenth, 0.0)
            for e, val in enumerate((total, fu, fd, fz[h], fzb[h], fn)):
                out[e, h] = val

    def bumps(near, far, face, edge, ghost, inside, there, bump, length, s1_, s2_):
        here, up, down = (shifted_rows(near, length, s) for s in (0, 1, -1))
        right, left = sideways(here, 1), sideways(here, -1)
        beyond = shifted_rows(far, length, 0)
        one = [-(face[h] * here[h]) for h in halves]
        for h in halves:
            bump[h, pl.ds(SUBS, length), :] = one[h]
        one_right, one_left = sideways(one, 1), sideways(one, -1)
        one_up, one_down = shifted_rows(bump, length, 1), shifted_rows(bump, length, -1)
        two, three = [], []
        for h in halves:
            val = (ghost[0, h] - s1_) * here[h] - ghost[5, h] * beyond[h] - face[h] * edge(h)
            val = val - ghost[1, h] * up[h] - ghost[2, h] * down[h]
            val = (val - ghost[3, h] * right[h] - ghost[4, h] * left[h]) * there
            total, fu, fd, fz, fzb, fn = (inside(e, h) for e in range(6))
            new = (total - s2_) * one[h] - fu * one_up[h] - fd * one_down[h]
            new = new - fz * one_right[h] - fzb * one_left[h] - face[h] * val
            two.append(new)
            three.append(-(fn * one[h]))
        return one, two, three

    def x_coefs(side):
        at = plane_at(side)
        def inside(e, h):
            if e == 5:
                return cx[h, plane_at(side, 0 if side == 0 else 1), :]
            return (diag, cy, cyb, cz, czb)[e][h, at, :]
        return inside

    there_c = [jnp.where(e, 0.0, 1.0).astype(F32) for e in edge_c]
    there_r = [jnp.where(e, 0.0, 1.0).astype(F32) for e in edge_r]
    sums = {}
    for r in range(2):
        src, mid, dst = w[2 * r:2 * r + 3]
        shift_one, shift_two = NEWTON[2 * r] / SCALE, NEWTON[2 * r + 1] / SCALE
        copies = send_layers(r, src)
        if r == 0:
            for side in range(2):
                at = plane_at(side)
                diag[:, at, :] = diag[:, at, :] + cfx[side]
            for side in range(2):
                for h in halves:
                    diag[h, strided(side), :] = diag[h, strided(side), :] + cfy[side, h]
            sums[0, 0], = stencil(src, mid, shift_one, False, [(None, None)])
            stencil(mid, dst, shift_two, False, [])
            arrive(second)
            corner_rows([gyk.at[s, 0] for s in range(2)], [gxk.at[s, 0] for s in range(2)], gck)
            for side in range(2):
                ghost_coefs(gyk.at[side, 0], gyk.at[side, 1], cfy.at[side], nx, ghost_y.at[side])
                ghost_coefs(gxk.at[side, 0], gxk.at[side, 1], cfx.at[side], ny, ghost_x.at[side])
                for h in halves:
                    for e, ref in ((0, diag), (3, cz), (4, czb), (5, cyb if side else cy)):
                        own_y[side, e, h] = ref[h, strided(side), :]
                    own_y[side, 1, h] = cx[h, strided(side), :]
                    bump_y[h, along, :] = own_y[side, 1, h]
                for h in halves:
                    own_y[side, 2, h] = bump_y[h, pl.ds(SUBS - 1, nx), :]
        else:
            sums[2, 2], sums[1, 2] = stencil(src, mid, shift_one, False, [(None, None), (None, w[1])])
            sums[1, 1], sums[0, 1] = stencil(mid, dst, shift_two, False, [(w[1], w[1]), (w[1], w[0])])
        arrive(copies)
        gy = [gyw.at[r, s, 0] for s in range(2)]
        gx = [gxw.at[r, s, 0] for s in range(2)]
        corner_rows(gy, gx, gcw.at[r])
        for side in range(2):
            at, below = plane_at(side), plane_at(side, 1)
            one, two, three = bumps(
                gx[side], gxw.at[r, side, 1], cfx[side], lambda h: src[h, at, :],
                ghost_x.at[side], x_coefs(side), there_r[side], bump_x, ny, shift_one, shift_two)
            for h in halves:
                mid[h, at, :] = mid[h, at, :] + one[h]
                dst[h, at, :] = dst[h, at, :] + two[h]
                dst[h, below, :] = dst[h, below, :] + three[h]
        for side in range(2):
            one, two, three = bumps(
                gy[side], gyw.at[r, side, 1], cfy[side], lambda h: fyw[r, side, 0, h],
                ghost_y.at[side], lambda e, h: own_y[side, e, h], there_c[side], bump_y, nx,
                shift_one, shift_two)
            for h in halves:
                outer = dst[h, strided(side), :] + two[h]
                within = dst[h, strided(side, 1), :] + three[h]
                dst[h, strided(side), :] = outer
                dst[h, strided(side, 1), :] = within
                if r == 0:
                    fyw[1, side, 0, h] = outer
                    fyw[1, side, 1, h] = within
                mid[h, strided(side), :] = mid[h, strided(side), :] + one[h]
    sums[3, 3], sums[2, 3], sums[4, 4], sums[3, 4] = grams(
        [(w[3], w[3]), (w[3], w[2]), (w[4], w[4]), (w[4], w[3])])

    def exchange(buf, ssem, rsem, peers, value):
        here = len(peers)
        buf[here] = value
        for e, (dr, dc) in enumerate(peers):
            pltpu.make_async_remote_copy(
                src_ref=buf.at[here], dst_ref=buf.at[e], send_sem=ssem.at[0], recv_sem=rsem.at[0],
                device_id=device(dr, dc), device_id_type=MESH).start()
        whole = buf.at[pl.ds(0, here)]
        pltpu.make_async_copy(whole, whole, rsem.at[0]).wait()
        parts = [buf[i] for i in range(here + 1)]
        while len(parts) > 1:
            parts = [a + b for a, b in zip(parts[::2], parts[1::2])] + (
                parts[-1:] if len(parts) % 2 else [])
        return parts[0]

    def finish_sends(buf, ssem, peers):
        whole = buf.at[pl.ds(0, len(peers))]
        pltpu.make_async_copy(whole, whole, ssem.at[0]).wait()

    everyone = [(dr, dc) for dr in range(nrows) for dc in range(ncols)][1:]
    pair_row = lax.broadcasted_iota(jnp.int32, (16, LANES), 0)
    on_diag = pair_row == lax.broadcasted_iota(jnp.int32, (16, LANES), 1)
    gm[...] = jnp.zeros(gm.shape, F32)
    for e, pair in enumerate(SUMS):
        gm[e:e + 1, :] = jnp.sum(sums[pair], axis=0, keepdims=True)
    line = jnp.sum(jnp.where(on_diag, jnp.sum(gm[...], axis=1, keepdims=True), 0.0),
                   axis=0, keepdims=True)
    if one_stage:
        pl.semaphore_wait(in_sem, len(row_peers))
        line = exchange(g1, s1, r1, everyone, line)
    else:
        line = exchange(g1, s1, r1, col_peers, line)
        line = exchange(g2, s2, r2, row_peers, line)
    gm[...] = jnp.broadcast_to(
        jnp.sum(jnp.where(on_diag, line, 0.0), axis=1, keepdims=True), gm.shape)
    moments = {pair: gm[e:e + 1, :] for e, pair in enumerate(SUMS)}
    for gap in range(2, 5):
        for i in range(5 - gap):
            j = i + gap
            moments[i, j] = moments[i + 1, j - 1] + (
                (NEWTON[i] - NEWTON[j - 1]) / SCALE) * moments[i, j - 1]
            moments[i, j] = moments[i, j]
    gram_one = lambda i, j: moments[min(i, j), max(i, j)]
    low_one, inv_one = cholesky(gram_one, 5)
    linv_one = lower_inverse(low_one, inv_one, 5)
    half = {(i, j): add_up([linv_one[i, m] * gram_one(m, j) for m in range(i + 1)])
            for i in range(5) for j in range(i + 1)}
    gram_two = {(i, j): add_up([half[i, m] * linv_one[j, m] for m in range(j + 1)])
                for i in range(5) for j in range(i + 1)}
    low_two, inv_two = cholesky(lambda i, j: gram_two[i, j], 5)
    linv_two = lower_inverse(low_two, inv_two, 5)

    trans = {(i, j): add_up([linv_two[i, m] * linv_one[m, j] for m in range(j, i + 1)])
             for i in range(5) for j in range(i + 1)}
    rfac = {(i, j): add_up([low_two[m, i] * low_one[j, m] for m in range(i, j + 1)])
            for i in range(5) for j in range(i, 5)}
    shifted = {}
    for k in range(4):
        for i in range(k + 2):
            val = rfac[i, k + 1] * SCALE
            shifted[i, k] = val + rfac[i, k] * NEWTON[k] if i <= k else val
    hess = {(i, k): add_up([shifted[i, m] * trans[k, m] for m in range(max(i - 1, 0), k + 1)])
            for k in range(4) for i in range(k + 2)}
    target, inv_n = [rfac[0, 0]], []
    for k in range(4):
        top, bottom = hess[k, k], hess[k + 1, k]
        square = top * top + bottom * bottom
        inv_n.append(inv_sqrt(square))
        cosine, sine = top * inv_n[k], bottom * inv_n[k]
        for j in range(k + 1, 4):
            upper, under = hess[k, j], hess[k + 1, j]
            hess[k, j] = cosine * upper + sine * under
            hess[k + 1, j] = cosine * under - sine * upper
        target.append(-(sine * target[k]))
        target[k] = cosine * target[k]
    weights = [None] * 4
    for i in range(3, -1, -1):
        val = target[i]
        for m in range(i + 1, 4):
            val = val - hess[i, m] * weights[m]
        weights[i] = val * inv_n[i]

    root = math.sqrt(nrows * ncols * nx * ny * nz)
    for e, (j, i) in enumerate(PAIRS):
        coef_out[e:e + 1, :] = trans[i, j] * root
    for k in range(4):
        coef_out[16 + k:17 + k, :] = weights[k] * (1.0 / root)
    one_row = lax.broadcasted_iota(jnp.int32, (1, LANES), 1)
    for i in range(5):
        line = jnp.zeros((1, LANES), F32)
        column = [rfac[i, 0] if i == 0 else jnp.zeros((1, LANES), F32)]
        for j in range(1, 5):
            below = rfac[i, j] if j >= i else 0.0
            column.append(below - column[j - 1] * (SHIFTS[j - 1] / SCALE))
        for j in range(i, 5):
            line = jnp.where(one_row == j, column[j], line)
        coef_out[24 + i:25 + i, :] = line

    if one_stage:
        finish_sends(g1, s1, everyone)
    else:
        finish_sends(g1, s1, col_peers)
        finish_sends(g2, s2, row_peers)
    for has_target, copy in sent:
        @pl.when(has_target)
        def _(copy=copy):
            copy.wait_send()


def finish_kernel(sizes, w_ref, coef_ref, basis_hbm, rfac_ref, updated_hbm, stage, sems):
    count, nz, chunk = sizes
    trans = {(i, j): jnp.broadcast_to(coef_ref[e:e + 1, :], (SUBS, LANES))
             for e, (j, i) in enumerate(PAIRS)}
    weights = [jnp.broadcast_to(coef_ref[16 + k:17 + k, :], (SUBS, LANES)) for k in range(4)]
    rfac_ref[...] = coef_ref[24:29, 0:5]
    copies = []
    for part in range(count // chunk):
        start = part * chunk

        def body(n, carry):
            at = pl.ds(pl.multiple_of(start + n * SUBS, SUBS), SUBS)
            rows_in = pl.ds(pl.multiple_of(start + n * SUBS, SUBS) + OFF, SUBS)
            for h in range(nz // LANES):
                lanes = pl.ds(h * LANES, LANES)
                raw = [w_ref[k, h, rows_in, :] for k in range(5)]
                new = w_ref[5, h, rows_in, :]
                for i in range(5):
                    val = trans[i, 0] * raw[0]
                    for j in range(1, i + 1):
                        val = val + trans[i, j] * raw[j]
                    stage[i, at, lanes] = val
                    if i < 4:
                        new = new + weights[i] * val
                stage[5, at, lanes] = new
            return carry
        lax.fori_loop(0, chunk // SUBS, body, 0, unroll=2)
        rows = pl.ds(start, chunk)
        for i in range(6):
            dst = basis_hbm.at[i, rows, :] if i < 5 else updated_hbm.at[rows, :]
            copies.append(pltpu.make_async_copy(stage.at[i, rows, :], dst, sems.at[part, i]))
            copies[-1].start()
    for copy in copies:
        copy.wait()


def on_device(nrows, ncols, right_side, initial, conduct):
    nx, ny, nz = initial.shape
    nh, count = nz // LANES, nx * ny
    flat = [a.reshape(count, nz) for a in (right_side, initial, conduct)]
    dma = pltpu.SemaphoreType.DMA
    slots = nrows * ncols if nrows * ncols <= 64 else ncols
    field = pltpu.VMEM((nh, count, LANES), F32)
    padded = pltpu.VMEM((nh, OFF + count + ny, LANES), F32)
    ends = 2 * SUBS
    vectors, coefs = pl.pallas_call(
        functools.partial(cycle_kernel, (nrows, ncols, nx, ny, nz)),
        out_shape=(pltpu.VMEM((6, nh, OFF + count + ny, LANES), F32),
                   pltpu.VMEM((32, LANES), F32)),
        in_specs=[pl.BlockSpec(memory_space=pltpu.HBM)] * 3,
        out_specs=(pl.BlockSpec(memory_space=pltpu.VMEM), pl.BlockSpec(memory_space=pltpu.VMEM)),
        scratch_shapes=[
            padded, field, padded, padded, padded, padded, padded, padded,
            pltpu.VMEM((2, nh, ny, LANES), F32), pltpu.VMEM((2, nh, nx, LANES), F32),
            pltpu.VMEM((2, 2, nh, nx, LANES), F32), pltpu.VMEM((2, nh, nx, LANES), F32),
            pltpu.VMEM((2, 2, 2, nh, nx, LANES), F32),
            pltpu.VMEM((2, 2, nh, nx + ends, LANES), F32), pltpu.VMEM((2, nh, nx, LANES), F32),
            pltpu.VMEM((2, 2, 2, nh, nx + ends, LANES), F32),
            pltpu.VMEM((2, 2, nh, ny + ends, LANES), F32), pltpu.VMEM((2, nh, ny, LANES), F32),
            pltpu.VMEM((2, 2, 2, nh, ny + ends, LANES), F32),
            pltpu.VMEM((4, nh, 1, LANES), F32), pltpu.VMEM((2, 4, nh, 1, LANES), F32),
            pltpu.VMEM((4, nh, 1, LANES), F32), pltpu.VMEM((2, 4, nh, 1, LANES), F32),
            pltpu.VMEM((2, 6, nh, nx, LANES), F32), pltpu.VMEM((2, 6, nh, ny, LANES), F32),
            pltpu.VMEM((2, 6, nh, nx, LANES), F32),
            pltpu.VMEM((nh, nx + ends, LANES), F32), pltpu.VMEM((nh, ny + ends, LANES), F32),
            pltpu.VMEM((slots, 1, LANES), F32), pltpu.VMEM((nrows, 1, LANES), F32),
            pltpu.VMEM((16, LANES), F32),
            dma((3, nh)), dma((36,)), dma((36,)),
            dma((1,)), dma((1,)), dma((1,)), dma((1,)), pltpu.SemaphoreType.REGULAR,
        ],
        compiler_params=pltpu.CompilerParams(
            collective_id=0, has_side_effects=True, vmem_limit_bytes=57 << 20),
        name="cycle",
    )(*flat)
    chunk = min(128, count)
    basis, rfactor, updated = pl.pallas_call(
        functools.partial(finish_kernel, (count, nz, chunk)),
        out_shape=(jax.ShapeDtypeStruct((5, count, nz), F32),
                   jax.ShapeDtypeStruct((5, 5), F32),
                   jax.ShapeDtypeStruct((count, nz), F32)),
        in_specs=[pl.BlockSpec(memory_space=pltpu.VMEM)] * 2,
        out_specs=(pl.BlockSpec(memory_space=pltpu.HBM), pl.BlockSpec(memory_space=pltpu.VMEM),
                   pl.BlockSpec(memory_space=pltpu.HBM)),
        scratch_shapes=[pltpu.VMEM((6, count, nz), F32), dma((count // chunk, 6))],
        compiler_params=pltpu.CompilerParams(vmem_limit_bytes=20 << 20),
        name="finish",
    )(vectors, coefs)
    return (basis.reshape(5, nx, ny, nz), rfactor, updated.reshape(nx, ny, nz))


def solution(mesh):
    nrows, ncols = mesh.shape["rows"], mesh.shape["cols"]
    return jax.shard_map(
        functools.partial(on_device, nrows, ncols),
        mesh=mesh,
        in_specs=(P("rows", "cols", None),) * 3,
        out_specs=(P(None, "rows", "cols", None), P(), P("rows", "cols", None)),
        check_vma=False,
    )
```

```python
import functools
import math

import jax
import jax.numpy as jnp
from jax import lax
from jax.experimental import pallas as pl
from jax.experimental.pallas import tpu as pltpu
from jax.sharding import PartitionSpec as P

SHIFTS = (12.0, 3.0, 21.0, 7.0)
NEWTON = (0.0,) + SHIFTS[:3]
SCALE = 8.0
LANES = 128
SUBS = 8
PLANES = 8
OFF = SUBS
MESH = pl.DeviceIdType.MESH
PAIRS = [(i, j) for j in range(5) for i in range(j + 1)]
SUMS = [(0, 0)] + [(k - d, k) for k in range(1, 5) for d in (1, 0)]
F32 = jnp.float32


def inv_sqrt(value):
    guess = lax.rsqrt(value)
    return guess * (1.5 - 0.5 * (value * guess) * guess)


def cholesky(entry, order):
    lower, inv = {}, []
    for col in range(order):
        diag = entry(col, col)
        for inner in range(col):
            diag = diag - lower[col, inner] * lower[col, inner]
        root = inv_sqrt(diag)
        inv.append(root)
        lower[col, col] = diag * root
        for row in range(col + 1, order):
            val = entry(row, col)
            for inner in range(col):
                val = val - lower[row, inner] * lower[col, inner]
            lower[row, col] = val * root
    return lower, inv


def lower_inverse(lower, inv, order):
    result = {}
    for row in range(order):
        for col in range(row):
            total = lower[row, col] * result[col, col]
            for inner in range(col + 1, row):
                total = total + lower[row, inner] * result[inner, col]
            result[row, col] = -(total * inv[row])
        result[row, row] = inv[row]
    return result


def add_up(terms):
    return functools.reduce(lambda a, b: a + b, terms)


def cycle_kernel(sizes, rs_hbm, init_hbm, cond_hbm, w_out, coef_out,
                 kk, rs, diag, cx, cy, cyb, cz, czb, cfx, cfy,
                 fyk, fyu, fyw, fyp, fxp, gyk, gyu, gyw, gyp, gxk, gxu, gxw, gxp, ck, cw, gck, gcw,
                 corner_y, corner_x, own_y, two_y, two_x, bump_y, bump_x,
                 g1, g2, gm, load_sem, hs_sem, hr_sem, s1, r1, s2, r2, in_sem):
    nrows, ncols, nx, ny, nz = sizes
    nh, ng = nz // LANES, ny // SUBS
    count = nx * ny
    one_stage = nrows * ncols <= 64
    halves = range(nh)
    cells = [(h, g) for h in halves for g in range(ng)]
    me_r, me_c = lax.axis_index("rows"), lax.axis_index("cols")
    uu = w_out.at[5]
    w = [w_out.at[k] for k in range(5)]
    inner = pl.ds(OFF, count)

    loads = []
    for idx, (src, dst) in enumerate(((cond_hbm, kk), (init_hbm, uu), (rs_hbm, rs))):
        for h in halves:
            loads.append(pltpu.make_async_copy(
                src.at[:, pl.ds(h * LANES, LANES)],
                dst.at[h, inner if idx < 2 else pl.ds(0, count), :], load_sem.at[idx, h]))
            loads[-1].start()

    barrier = pltpu.get_barrier_semaphore()
    col_peers = [(0, d) for d in range(1, ncols)]
    row_peers = [(d, 0) for d in range(1, nrows)]
    greeted = col_peers + row_peers + sorted(
        {(dr % nrows, dc % ncols) for dr in (-1, 1) for dc in (-1, 1)}
        - set(col_peers + row_peers + [(0, 0)]))

    def device(dr, dc):
        return (lax.rem(me_r + dr, nrows), lax.rem(me_c + dc, ncols))

    for dr, dc in greeted:
        pl.semaphore_signal(barrier, inc=1, device_id_type=MESH, device_id=device(dr, dc))

    for ref in [kk] + [w_out.at[i] for i in range(6)]:
        ref[:, pl.ds(0, OFF), :] = jnp.zeros((nh, OFF, LANES), F32)
        ref[:, pl.ds(OFF + count, ny), :] = jnp.zeros((nh, ny, LANES), F32)
    for ref, length in ((bump_y, nx), (bump_x, ny)):
        for row in (0, SUBS + length):
            ref[:, pl.ds(row, SUBS), :] = jnp.zeros((nh, SUBS, LANES), F32)
    edge_c, edge_r = (me_c == 0, me_c == ncols - 1), (me_r == 0, me_r == nrows - 1)
    for side in range(2):
        @pl.when(edge_c[side])
        def _(side=side):
            for ref in (gyk.at[side], gyu.at[side], gyw.at[0, side], gyw.at[1, side],
                        gyp.at[0, side], gyp.at[1, side]):
                ref[...] = jnp.zeros(ref.shape, F32)

        @pl.when(edge_r[side])
        def _(side=side):
            for ref in (gxk.at[side], gxu.at[side], gxw.at[0, side], gxw.at[1, side],
                        gxp.at[0, side], gxp.at[1, side]):
                ref[...] = jnp.zeros(ref.shape, F32)
        for other in range(2):
            @pl.when(jnp.logical_or(edge_r[side], edge_c[other]))
            def _(q=2 * side + other):
                for ref in (gck.at[q], gcw.at[0, q], gcw.at[1, q]):
                    ref[...] = jnp.zeros(ref.shape, F32)

    sent = []

    def transfer(src, dst, dr, dc):
        def exists(step_r, step_c):
            tests = []
            if step_r:
                tests.append(me_r < nrows - 1 if step_r > 0 else me_r > 0)
            if step_c:
                tests.append(me_c < ncols - 1 if step_c > 0 else me_c > 0)
            return functools.reduce(jnp.logical_and, tests)
        n = len(sent)
        copy = pltpu.make_async_remote_copy(
            src_ref=src, dst_ref=dst, send_sem=hs_sem.at[n], recv_sem=hr_sem.at[n],
            device_id=(me_r + dr, me_c + dc), device_id_type=MESH)
        has_target = exists(dr, dc)
        sent.append((has_target, copy))

        @pl.when(has_target)
        def _():
            copy.start()
        return exists(-dr, -dc), copy

    def arrive(copies):
        for has_source, copy in copies:
            @pl.when(has_source)
            def _(copy=copy):
                copy.wait_recv()

    def toward(side):
        return 1 if side == 0 else -1

    def strided(side, depth=0):
        return pl.ds(OFF + (depth if side == 0 else ny - 1 - depth), nx, stride=ny)

    def plane_at(side, depth=0):
        return pl.ds(OFF + (depth if side == 0 else nx - 1 - depth) * ny, ny)

    def corner_at(q):
        return pl.ds(OFF + (q // 2) * (nx - 1) * ny + (q % 2) * (ny - 1), 1)

    along = pl.ds(SUBS, nx)
    across = pl.ds(SUBS, ny)

    def send_corners(ref, mine, theirs):
        made = []
        for q in range(4):
            mine[q] = ref[:, corner_at(q), :]
        for q in range(4):
            made.append(transfer(mine.at[3 - q], theirs.at[q], toward(q // 2), toward(q % 2)))
        return made

    for cp in loads[:2 * nh]:
        cp.wait()
    for side in range(2):
        for h in halves:
            fyk[side, h] = kk[h, strided(side), :]
            fyu[side, h] = uu[h, strided(side), :]
    pl.semaphore_wait(barrier, len(greeted))
    first = []
    for side in range(2):
        t = toward(side)
        first.append(transfer(fyk.at[1 - side], gyk.at[side], 0, t))
        first.append(transfer(fyu.at[1 - side], gyu.at[side], 0, t))
    for side in range(2):
        t = toward(side)
        first.append(transfer(kk.at[:, plane_at(1 - side), :], gxk.at[side], t, 0))
        first.append(transfer(uu.at[:, plane_at(1 - side), :], gxu.at[side], t, 0))
    second = send_corners(kk, ck, gck)
    if one_stage:
        for dr, dc in row_peers:
            pl.semaphore_signal(in_sem, inc=1, device_id_type=MESH, device_id=device(dr, dc))

    lane = lax.broadcasted_iota(jnp.int32, (SUBS, LANES), 1)
    sub = lax.broadcasted_iota(jnp.int32, (SUBS, LANES), 0)
    first_lane, last_lane = lane == 0, lane == LANES - 1
    first_sub, last_sub = sub == 0, sub == SUBS - 1
    zero = jnp.zeros((SUBS, LANES), F32)
    sixteenth = 0.5 / SCALE

    def tile(ref, h, g, base, offset=0):
        return ref[h, pl.ds(base + (g * SUBS + offset), SUBS), :]

    def get(ref, base, offset=0):
        return {(h, g): tile(ref, h, g, base, offset) for h, g in cells}

    def put(ref, base, values):
        for h, g in cells:
            ref[h, pl.ds(base + g * SUBS, SUBS), :] = values[h, g]

    def y_down(v):
        r = {c: pltpu.roll(v[c], 1, 0) for c in cells}
        return {(h, g): jnp.where(first_sub, r[h, g - 1], r[h, g]) if g > 0 else r[h, g]
                for h, g in cells}

    def z_up(v):
        r = {c: pltpu.roll(v[c], LANES - 1, 1) for c in v}
        return {(h, g): jnp.where(last_lane, r[h + 1, g], r[h, g]) if h < nh - 1 else r[h, g]
                for h, g in v}

    def z_down(v):
        r = {c: pltpu.roll(v[c], 1, 1) for c in v}
        return {(h, g): jnp.where(first_lane, r[h - 1, g], r[h, g]) if h > 0 else r[h, g]
                for h, g in v}

    flat = lambda v: tuple(v[c] for c in cells)
    dict_of = lambda t: dict(zip(cells, t))

    def coef_body(i, carry):
        here, cx_before = dict_of(carry[0]), dict_of(carry[1])
        for q in range(PLANES):
            low = pl.multiple_of((i * PLANES + q) * ny, ny)
            base = low + OFF
            after = get(kk, base + ny)
            up, right = get(kk, base, 1), z_up(here)
            fx = {c: (here[c] + after[c]) * sixteenth for c in cells}
            fy_ = {c: (here[c] + up[c]) * sixteenth for c in cells}
            fz = {c: (here[c] + right[c]) * sixteenth for c in cells}
            for h in halves:
                fy_[h, ng - 1] = jnp.where(last_sub, 0.0, fy_[h, ng - 1])
            for g in range(ng):
                fz[nh - 1, g] = jnp.where(last_lane, 0.0, fz[nh - 1, g])
            fyb, fzb = y_down(fy_), z_down(fz)
            for h in halves:
                fyb[h, 0] = jnp.where(first_sub, 0.0, fyb[h, 0])
            for g in range(ng):
                fzb[0, g] = jnp.where(first_lane, 0.0, fzb[0, g])
            total = {c: ((fx[c] + cx_before[c]) + (fy_[c] + fyb[c])) + (fz[c] + fzb[c])
                     for c in cells}
            for g in range(ng):
                total[0, g] = total[0, g] + jnp.where(first_lane, here[0, g] * sixteenth, 0.0)
                total[nh - 1, g] = total[nh - 1, g] + jnp.where(
                    last_lane, here[nh - 1, g] * sixteenth, 0.0)
            for ref, val in ((cx, fx), (cy, fy_), (cyb, fyb), (cz, fz), (czb, fzb), (diag, total)):
                put(ref, base, val)
            here, cx_before = after, fx
        return flat(here), flat(cx_before)

    lax.fori_loop(0, nx // PLANES, coef_body, (flat(get(kk, OFF)), (zero,) * len(cells)))
    last = OFF + count - ny
    put(diag, last, {c: tile(diag, *c, last) - tile(cx, *c, last) for c in cells})
    put(cx, last, {c: zero for c in cells})

    def products(accs, pairs, here, base):
        for acc, (one, two) in zip(accs, pairs):
            for c in cells:
                left = here[c] if one is None else tile(one, *c, base)
                right = here[c] if two is None else tile(two, *c, base)
                acc[c] = acc[c] + left * right

    def stencil(src, dst, shift, residual, pairs):
        def body(i, carry):
            here, before, cx_before = (dict_of(t) for t in carry[:3])
            accs = [dict_of(t) for t in carry[3]]
            for q in range(PLANES):
                low = pl.multiple_of((i * PLANES + q) * ny, ny)
                base = low + OFF
                after = get(src, base + ny)
                up, down, right, left = get(src, base, 1), get(src, base, -1), z_up(here), z_down(here)
                new = {}
                fx = get(cx, base)
                for c in cells:
                    d = tile(diag, *c, base)
                    val = (d - shift if shift else d) * here[c]
                    val = val - fx[c] * after[c]
                    val = val - cx_before[c] * before[c]
                    val = val - tile(cy, *c, base) * up[c]
                    val = val - tile(cyb, *c, base) * down[c]
                    val = val - tile(cz, *c, base) * right[c]
                    val = val - tile(czb, *c, base) * left[c]
                    if residual:
                        val = tile(rs, *c, low) - SCALE * val
                    new[c] = val
                products(accs, pairs, here, base)
                put(dst, base, new)
                before, here, cx_before = here, after, fx
            return flat(here), flat(before), flat(cx_before), tuple(flat(a) for a in accs)
        nothing = (zero,) * len(cells)
        out = lax.fori_loop(0, nx // PLANES, body,
                            (flat(get(src, OFF)), nothing, nothing, (nothing,) * len(pairs)))
        return [add_up(list(t)) for t in out[3]]

    def grams(pairs):
        def body(i, carry):
            accs = [dict_of(t) for t in carry]
            for q in range(PLANES):
                low = pl.multiple_of((i * PLANES + q) * ny, ny)
                products(accs, pairs, None, low + OFF)
            return tuple(flat(a) for a in accs)
        out = lax.fori_loop(0, nx // PLANES, body, ((zero,) * len(cells),) * len(pairs))
        return [add_up(list(t)) for t in out]

    for cp in loads[2 * nh:]:
        cp.wait()
    stencil(uu, w[0], 0.0, True, [])
    for side in range(2):
        for h in halves:
            for e, ref in ((3, cz), (4, czb), (5, cyb if side else cy), (1, cx)):
                own_y[side, e, h] = ref[h, strided(side), :]
            bump_y[h, along, :] = own_y[side, 1, h]
        for h in halves:
            own_y[side, 2, h] = bump_y[h, pl.ds(SUBS - 1, nx), :]
    arrive(first)
    for side in range(2):
        at = plane_at(side)
        coef = (kk[:, at, :] + gxk[side]) * sixteenth
        cfx[side] = coef
        w[0][:, at, :] = w[0][:, at, :] - SCALE * (coef * (uu[:, at, :] - gxu[side]))
    for side in range(2):
        for h in halves:
            coef = (fyk[side, h] + gyk[side, h]) * sixteenth
            cfy[side, h] = coef
            new = w[0][h, strided(side), :] - SCALE * (coef * (fyu[side, h] - gyu[side, h]))
            w[0][h, strided(side), :] = new
            fyw[0, side, h] = new

    def send_near(r, ref):
        made = []
        for side in range(2):
            made.append(transfer(fyw.at[r, 1 - side], gyw.at[r, side], 0, toward(side)))
        for side in range(2):
            made.append(transfer(ref.at[:, plane_at(1 - side), :], gxw.at[r, side], toward(side), 0))
        return made, send_corners(ref, cw.at[r], gcw.at[r])

    def send_next(r):
        made = []
        for side in range(2):
            made.append(transfer(fyp.at[r, 1 - side], gyp.at[r, side], 0, toward(side)))
        for side in range(2):
            made.append(transfer(fxp.at[r, 1 - side], gxp.at[r, side], toward(side), 0))
        return made

    def sideways(values, step):
        length = values[0].shape[0]
        index = lax.broadcasted_iota(jnp.int32, (length, LANES), 1)
        rolled = [pltpu.roll(v, LANES - 1 if step > 0 else 1, 1) for v in values]
        made = []
        for h in halves:
            if step > 0 and h < nh - 1:
                made.append(jnp.where(index == LANES - 1, rolled[h + 1], rolled[h]))
            elif step < 0 and h > 0:
                made.append(jnp.where(index == 0, rolled[h - 1], rolled[h]))
            else:
                made.append(rolled[h])
        return made

    def shifted_rows(ref, length, step):
        return [ref[h, pl.ds(SUBS + step, length), :] for h in halves]

    def in_plane(values, inside, shift, bump, length):
        for h in halves:
            bump[h, pl.ds(SUBS, length), :] = values[h]
        right, left = sideways(values, 1), sideways(values, -1)
        up, down = shifted_rows(bump, length, 1), shifted_rows(bump, length, -1)
        made = []
        for h in halves:
            total, fu, fd, fz, fzb = (inside(e, h) for e in range(5))
            val = (total - shift) * values[h] - fu * up[h] - fd * down[h]
            made.append(val - fz * right[h] - fzb * left[h])
        return made

    def x_coefs(side):
        at = plane_at(side)
        def inside(e, h):
            if e == 5:
                return cx[h, plane_at(side, 0 if side == 0 else 1), :]
            return (diag, cy, cyb, cz, czb)[e][h, at, :]
        return inside

    def y_coefs(side):
        return lambda e, h: own_y[side, e, h]

    there_c = [jnp.where(e, 0.0, 1.0).astype(F32) for e in edge_c]
    there_r = [jnp.where(e, 0.0, 1.0).astype(F32) for e in edge_r]

    def next_planes(r, src, shift):
        for side in range(2):
            within = [src[h, strided(side, 1), :] for h in halves]
            val = in_plane([fyw[r, side, h] for h in halves], y_coefs(side), shift, bump_y, nx)
            for h in halves:
                fyp[r, side, h] = val[h] - own_y[side, 5, h] * within[h]
        for side in range(2):
            at, below = plane_at(side), plane_at(side, 1)
            inside = x_coefs(side)
            val = in_plane([src[h, at, :] for h in halves], inside, shift, bump_x, ny)
            for h in halves:
                fxp[r, side, h] = val[h] - inside(5, h) * src[h, below, :]

    def mend(mid, r):
        for side in range(2):
            at = plane_at(side)
            for h in halves:
                mid[h, at, :] = mid[h, at, :] + gxw[r, side, h]
        for side in range(2):
            for h in halves:
                mid[h, strided(side), :] = mid[h, strided(side), :] + gyw[r, side, h]

    sums = {}
    for r in range(2):
        src, mid, dst = w[2 * r:2 * r + 3]
        shift_one, shift_two = NEWTON[2 * r] / SCALE, NEWTON[2 * r + 1] / SCALE
        near, corners = send_near(r, src)
        if r == 0:
            for side in range(2):
                at = plane_at(side)
                diag[:, at, :] = diag[:, at, :] + cfx[side]
            for side in range(2):
                for h in halves:
                    own_y[side, 0, h] = diag[h, strided(side), :] + cfy[side, h]
                    diag[h, strided(side), :] = own_y[side, 0, h]
        next_planes(r, src, shift_one)
        far = send_next(r)
        if r == 0:
            sums[0, 0], = stencil(src, mid, shift_one, False, [(None, None)])
            stencil(mid, dst, shift_two, False, [])
            arrive(second)
            for side in range(2):
                for end in range(2):
                    q = 2 * end + side
                    corner_y[side, end] = (gck[q] + gyk[side, :, pl.ds(end * (nx - 1), 1), :]) * sixteenth
                    q = 2 * side + end
                    corner_x[side, end] = (gck[q] + gxk[side, :, pl.ds(end * (ny - 1), 1), :]) * sixteenth
        else:
            mend(w[1], 0)
            sums[2, 2], sums[1, 2] = stencil(src, mid, shift_one, False, [(None, None), (None, w[1])])
            sums[1, 1], sums[0, 1] = stencil(mid, dst, shift_two, False, [(w[1], w[1]), (w[1], w[0])])
        arrive(near)
        for side in range(2):
            for axis, ghost, face, inside, bump, length in (
                    ("x", gxw.at[r, side], cfx.at[side], x_coefs(side), bump_x, ny),
                    ("y", gyw.at[r, side], cfy.at[side], y_coefs(side), bump_y, nx)):
                one = [-(face[h] * ghost[h]) for h in halves]
                two = in_plane(one, inside, shift_two, bump, length)
                for h in halves:
                    ghost[h] = one[h]
                    if axis == "x":
                        two_x[side, h] = two[h]
                    else:
                        two_y[side, h] = two[h]
        arrive(corners)
        arrive(far)
        for side in range(2):
            for end in range(2):
                at = pl.ds(end * (nx - 1), 1)
                gyp[r, side, :, at, :] = (
                    gyp[r, side, :, at, :] - corner_y[side, end] * gcw[r, 2 * end + side])
                at = pl.ds(end * (ny - 1), 1)
                gxp[r, side, :, at, :] = (
                    gxp[r, side, :, at, :] - corner_x[side, end] * gcw[r, 2 * side + end])
        for side in range(2):
            at, below = plane_at(side), plane_at(side, 1)
            inside = x_coefs(side)
            for h in halves:
                val = (gxp[r, side, h] - cfx[side, h] * src[h, at, :]) * there_r[side]
                dst[h, at, :] = dst[h, at, :] + (two_x[side, h] - cfx[side, h] * val)
                dst[h, below, :] = dst[h, below, :] - inside(5, h) * gxw[r, side, h]
        for side in range(2):
            for h in halves:
                val = (gyp[r, side, h] - cfy[side, h] * fyw[r, side, h]) * there_c[side]
                outer = dst[h, strided(side), :] + (two_y[side, h] - cfy[side, h] * val)
                within = dst[h, strided(side, 1), :] - own_y[side, 5, h] * gyw[r, side, h]
                dst[h, strided(side), :] = outer
                dst[h, strided(side, 1), :] = within
                if r == 0:
                    fyw[1, side, h] = outer
        if r == 1:
            mend(w[3], 1)

    sums[3, 3], sums[2, 3], sums[4, 4], sums[3, 4] = grams(
        [(w[3], w[3]), (w[3], w[2]), (w[4], w[4]), (w[4], w[3])])

    def exchange(buf, ssem, rsem, peers, value):
        here = len(peers)
        buf[here] = value
        for e, (dr, dc) in enumerate(peers):
            pltpu.make_async_remote_copy(
                src_ref=buf.at[here], dst_ref=buf.at[e], send_sem=ssem.at[0], recv_sem=rsem.at[0],
                device_id=device(dr, dc), device_id_type=MESH).start()
        whole = buf.at[pl.ds(0, here)]
        pltpu.make_async_copy(whole, whole, rsem.at[0]).wait()
        parts = [buf[i] for i in range(here + 1)]
        while len(parts) > 1:
            parts = [a + b for a, b in zip(parts[::2], parts[1::2])] + (
                parts[-1:] if len(parts) % 2 else [])
        return parts[0]

    def finish_sends(buf, ssem, peers):
        whole = buf.at[pl.ds(0, len(peers))]
        pltpu.make_async_copy(whole, whole, ssem.at[0]).wait()

    everyone = [(dr, dc) for dr in range(nrows) for dc in range(ncols)][1:]
    pair_row = lax.broadcasted_iota(jnp.int32, (16, LANES), 0)
    on_diag = pair_row == lax.broadcasted_iota(jnp.int32, (16, LANES), 1)
    gm[...] = jnp.zeros(gm.shape, F32)
    for e, pair in enumerate(SUMS):
        gm[e:e + 1, :] = jnp.sum(sums[pair], axis=0, keepdims=True)
    line = jnp.sum(jnp.where(on_diag, jnp.sum(gm[...], axis=1, keepdims=True), 0.0),
                   axis=0, keepdims=True)
    if one_stage:
        pl.semaphore_wait(in_sem, len(row_peers))
        line = exchange(g1, s1, r1, everyone, line)
    else:
        line = exchange(g1, s1, r1, col_peers, line)
        line = exchange(g2, s2, r2, row_peers, line)
    gm[...] = jnp.broadcast_to(
        jnp.sum(jnp.where(on_diag, line, 0.0), axis=1, keepdims=True), gm.shape)
    moments = {pair: gm[e:e + 1, :] for e, pair in enumerate(SUMS)}
    for gap in range(2, 5):
        for i in range(5 - gap):
            j = i + gap
            moments[i, j] = moments[i + 1, j - 1] + (
                (NEWTON[i] - NEWTON[j - 1]) / SCALE) * moments[i, j - 1]
            moments[i, j] = moments[i, j]
    gram_one = lambda i, j: moments[min(i, j), max(i, j)]
    low_one, inv_one = cholesky(gram_one, 5)
    linv_one = lower_inverse(low_one, inv_one, 5)
    half = {(i, j): add_up([linv_one[i, m] * gram_one(m, j) for m in range(i + 1)])
            for i in range(5) for j in range(i + 1)}
    gram_two = {(i, j): add_up([half[i, m] * linv_one[j, m] for m in range(j + 1)])
                for i in range(5) for j in range(i + 1)}
    low_two, inv_two = cholesky(lambda i, j: gram_two[i, j], 5)
    linv_two = lower_inverse(low_two, inv_two, 5)

    trans = {(i, j): add_up([linv_two[i, m] * linv_one[m, j] for m in range(j, i + 1)])
             for i in range(5) for j in range(i + 1)}
    rfac = {(i, j): add_up([low_two[m, i] * low_one[j, m] for m in range(i, j + 1)])
            for i in range(5) for j in range(i, 5)}
    shifted = {}
    for k in range(4):
        for i in range(k + 2):
            val = rfac[i, k + 1] * SCALE
            shifted[i, k] = val + rfac[i, k] * NEWTON[k] if i <= k else val
    hess = {(i, k): add_up([shifted[i, m] * trans[k, m] for m in range(max(i - 1, 0), k + 1)])
            for k in range(4) for i in range(k + 2)}
    target, inv_n = [rfac[0, 0]], []
    for k in range(4):
        top, bottom = hess[k, k], hess[k + 1, k]
        square = top * top + bottom * bottom
        inv_n.append(inv_sqrt(square))
        cosine, sine = top * inv_n[k], bottom * inv_n[k]
        for j in range(k + 1, 4):
            upper, under = hess[k, j], hess[k + 1, j]
            hess[k, j] = cosine * upper + sine * under
            hess[k + 1, j] = cosine * under - sine * upper
        target.append(-(sine * target[k]))
        target[k] = cosine * target[k]
    weights = [None] * 4
    for i in range(3, -1, -1):
        val = target[i]
        for m in range(i + 1, 4):
            val = val - hess[i, m] * weights[m]
        weights[i] = val * inv_n[i]

    root = math.sqrt(nrows * ncols * nx * ny * nz)
    for e, (j, i) in enumerate(PAIRS):
        coef_out[e:e + 1, :] = trans[i, j] * root
    for k in range(4):
        coef_out[16 + k:17 + k, :] = weights[k] * (1.0 / root)
    one_row = lax.broadcasted_iota(jnp.int32, (1, LANES), 1)
    for i in range(5):
        line = jnp.zeros((1, LANES), F32)
        column = [rfac[i, 0] if i == 0 else jnp.zeros((1, LANES), F32)]
        for j in range(1, 5):
            below = rfac[i, j] if j >= i else 0.0
            column.append(below - column[j - 1] * (SHIFTS[j - 1] / SCALE))
        for j in range(i, 5):
            line = jnp.where(one_row == j, column[j], line)
        coef_out[24 + i:25 + i, :] = line

    if one_stage:
        finish_sends(g1, s1, everyone)
    else:
        finish_sends(g1, s1, col_peers)
        finish_sends(g2, s2, row_peers)
    for has_target, copy in sent:
        @pl.when(has_target)
        def _(copy=copy):
            copy.wait_send()


def finish_kernel(parts, nz, w_ref, coef_ref, basis_hbm, rfac_ref, updated_hbm, stage, last, sems):
    trans = {(i, j): jnp.broadcast_to(coef_ref[e:e + 1, :], (SUBS, LANES))
             for e, (j, i) in enumerate(PAIRS)}
    weights = [jnp.broadcast_to(coef_ref[16 + k:17 + k, :], (SUBS, LANES)) for k in range(4)]
    rfac_ref[...] = coef_ref[24:29, 0:5]
    copies = []
    for part, (start, size) in enumerate(parts):

        def body(n, carry):
            low = pl.multiple_of(start + n * SUBS, SUBS)
            at, rows_in = pl.ds(low, SUBS), pl.ds(low + OFF, SUBS)
            for h in range(nz // LANES):
                lanes = pl.ds(h * LANES, LANES)
                raw = [w_ref[k, h, rows_in, :] for k in range(5)]
                new = w_ref[5, h, rows_in, :]
                for i in range(5):
                    val = trans[i, 0] * raw[0]
                    for j in range(1, i + 1):
                        val = val + trans[i, j] * raw[j]
                    stage[i, at, lanes] = val
                    if i < 4:
                        new = new + weights[i] * val
                last[at, lanes] = new
            return carry
        lax.fori_loop(0, size // SUBS, body, 0, unroll=8)
        rows = pl.ds(start, size)
        for e, (src, dst) in enumerate(((stage.at[:, rows, :], basis_hbm.at[:, rows, :]),
                                        (last.at[rows, :], updated_hbm.at[rows, :]))):
            copies.append(pltpu.make_async_copy(src, dst, sems.at[part, e]))
            copies[-1].start()
    for copy in copies:
        copy.wait()


def on_device(nrows, ncols, right_side, initial, conduct):
    nx, ny, nz = initial.shape
    nh, count = nz // LANES, nx * ny
    flat = [a.reshape(count, nz) for a in (right_side, initial, conduct)]
    dma = pltpu.SemaphoreType.DMA
    slots = nrows * ncols if nrows * ncols <= 64 else ncols
    field = pltpu.VMEM((nh, count, LANES), F32)
    padded = pltpu.VMEM((nh, OFF + count + ny, LANES), F32)
    ends = 2 * SUBS
    y_pair, x_pair = pltpu.VMEM((2, nh, nx, LANES), F32), pltpu.VMEM((2, nh, ny, LANES), F32)
    y_four, x_four = pltpu.VMEM((2, 2, nh, nx, LANES), F32), pltpu.VMEM((2, 2, nh, ny, LANES), F32)
    vectors, coefs = pl.pallas_call(
        functools.partial(cycle_kernel, (nrows, ncols, nx, ny, nz)),
        out_shape=(pltpu.VMEM((6, nh, OFF + count + ny, LANES), F32),
                   pltpu.VMEM((32, LANES), F32)),
        in_specs=[pl.BlockSpec(memory_space=pltpu.HBM)] * 3,
        out_specs=(pl.BlockSpec(memory_space=pltpu.VMEM), pl.BlockSpec(memory_space=pltpu.VMEM)),
        scratch_shapes=[
            padded, field, padded, padded, padded, padded, padded, padded,
            pltpu.VMEM((2, nh, ny, LANES), F32), pltpu.VMEM((2, nh, nx, LANES), F32),
            y_pair, y_pair, y_four, y_four, x_four, y_pair, y_pair, y_four, y_four,
            x_pair, x_pair, x_four, x_four,
            pltpu.VMEM((4, nh, 1, LANES), F32), pltpu.VMEM((2, 4, nh, 1, LANES), F32),
            pltpu.VMEM((4, nh, 1, LANES), F32), pltpu.VMEM((2, 4, nh, 1, LANES), F32),
            pltpu.VMEM((2, 2, nh, 1, LANES), F32), pltpu.VMEM((2, 2, nh, 1, LANES), F32),
            pltpu.VMEM((2, 6, nh, nx, LANES), F32), y_pair, x_pair,
            pltpu.VMEM((nh, nx + ends, LANES), F32), pltpu.VMEM((nh, ny + ends, LANES), F32),
            pltpu.VMEM((slots, 1, LANES), F32), pltpu.VMEM((nrows, 1, LANES), F32),
            pltpu.VMEM((16, LANES), F32),
            dma((3, nh)), dma((36,)), dma((36,)),
            dma((1,)), dma((1,)), dma((1,)), dma((1,)), pltpu.SemaphoreType.REGULAR,
        ],
        compiler_params=pltpu.CompilerParams(
            collective_id=0, has_side_effects=True, vmem_limit_bytes=57 << 20),
        name="cycle",
    )(*flat)
    unit = count // 16
    sizes = [unit * n for n in (1, 3, 4, 4, 3, 1)]
    parts = [(sum(sizes[:i]), size) for i, size in enumerate(sizes)]
    basis, rfactor, updated = pl.pallas_call(
        functools.partial(finish_kernel, parts, nz),
        out_shape=(jax.ShapeDtypeStruct((5, count, nz), F32),
                   jax.ShapeDtypeStruct((5, 5), F32),
                   jax.ShapeDtypeStruct((count, nz), F32)),
        in_specs=[pl.BlockSpec(memory_space=pltpu.VMEM)] * 2,
        out_specs=(pl.BlockSpec(memory_space=pltpu.HBM), pl.BlockSpec(memory_space=pltpu.VMEM),
                   pl.BlockSpec(memory_space=pltpu.HBM)),
        scratch_shapes=[pltpu.VMEM((5, count, nz), F32), pltpu.VMEM((count, nz), F32),
                        dma((len(parts), 2))],
        compiler_params=pltpu.CompilerParams(vmem_limit_bytes=20 << 20),
        name="finish",
    )(vectors, coefs)
    return (basis.reshape(5, nx, ny, nz), rfactor, updated.reshape(nx, ny, nz))


def solution(mesh):
    nrows, ncols = mesh.shape["rows"], mesh.shape["cols"]
    return jax.shard_map(
        functools.partial(on_device, nrows, ncols),
        mesh=mesh,
        in_specs=(P("rows", "cols", None),) * 3,
        out_specs=(P(None, "rows", "cols", None), P(), P("rows", "cols", None)),
        check_vma=False,
    )
```

```python
import functools
import math

import jax
import jax.numpy as jnp
from jax import lax
from jax.experimental import pallas as pl
from jax.experimental.pallas import tpu as pltpu
from jax.sharding import PartitionSpec as P

SHIFTS = (12.0, 3.0, 21.0, 7.0)
NEWTON = (0.0,) + SHIFTS[:3]
SCALE = 8.0
LANES = 128
SUBS = 8
PLANES = 8
OFF = SUBS
MESH = pl.DeviceIdType.MESH
PAIRS = [(i, j) for j in range(5) for i in range(j + 1)]
SUMS = [(0, 0)] + [(k - d, k) for k in range(1, 5) for d in (1, 0)]
F32 = jnp.float32


def inv_sqrt(value):
    guess = lax.rsqrt(value)
    return guess * (1.5 - 0.5 * (value * guess) * guess)


def cholesky(entry, order):
    lower, inv = {}, []
    for col in range(order):
        diag = entry(col, col)
        for inner in range(col):
            diag = diag - lower[col, inner] * lower[col, inner]
        root = inv_sqrt(diag)
        inv.append(root)
        lower[col, col] = diag * root
        for row in range(col + 1, order):
            val = entry(row, col)
            for inner in range(col):
                val = val - lower[row, inner] * lower[col, inner]
            lower[row, col] = val * root
    return lower, inv


def lower_inverse(lower, inv, order):
    result = {}
    for row in range(order):
        for col in range(row):
            total = lower[row, col] * result[col, col]
            for inner in range(col + 1, row):
                total = total + lower[row, inner] * result[inner, col]
            result[row, col] = -(total * inv[row])
        result[row, row] = inv[row]
    return result


def add_up(terms):
    return functools.reduce(lambda a, b: a + b, terms)


def cycle_kernel(sizes, rs_hbm, init_hbm, cond_hbm, w_out, coef_out,
                 kk, rs, diag, cx, cy, cyb, cz, czb, cfx, cfy,
                 fyk, fyu, fyw, fyp, fxp, gyk, gyu, gyw, gyp, gxk, gxu, gxw, gxp, ck, cw, gck, gcw,
                 corner_y, corner_x, own_y, two_y, inner_y, outer_y, bump_y, bump_x,
                 g1, g2, gm, load_sem, hs_sem, hr_sem, s1, r1, s2, r2, in_sem):
    nrows, ncols, nx, ny, nz = sizes
    nh, ng = nz // LANES, ny // SUBS
    count = nx * ny
    one_stage = nrows * ncols <= 64
    halves = range(nh)
    cells = [(h, g) for h in halves for g in range(ng)]
    me_r, me_c = lax.axis_index("rows"), lax.axis_index("cols")
    uu = w_out.at[5]
    w = [w_out.at[k] for k in range(5)]
    inner = pl.ds(OFF, count)

    barrier = pltpu.get_barrier_semaphore()
    col_peers = [(0, d) for d in range(1, ncols)]
    row_peers = [(d, 0) for d in range(1, nrows)]
    greeted = col_peers + row_peers + sorted(
        {(dr % nrows, dc % ncols) for dr in (-1, 1) for dc in (-1, 1)}
        - set(col_peers + row_peers + [(0, 0)]))

    def device(dr, dc):
        return (lax.rem(me_r + dr, nrows), lax.rem(me_c + dc, ncols))

    for dr, dc in greeted:
        pl.semaphore_signal(barrier, inc=1, device_id_type=MESH, device_id=device(dr, dc))

    loads = []
    for idx, (src, dst) in enumerate(((cond_hbm, kk), (init_hbm, uu), (rs_hbm, rs))):
        for h in halves:
            loads.append(pltpu.make_async_copy(
                src.at[:, pl.ds(h * LANES, LANES)],
                dst.at[h, inner if idx < 2 else pl.ds(0, count), :], load_sem.at[idx, h]))
            loads[-1].start()

    for ref in [kk] + [w_out.at[i] for i in range(6)]:
        ref[:, pl.ds(0, OFF), :] = jnp.zeros((nh, OFF, LANES), F32)
        ref[:, pl.ds(OFF + count, ny), :] = jnp.zeros((nh, ny, LANES), F32)
    for ref, length in ((bump_y, nx), (bump_x, ny)):
        for row in (0, SUBS + length):
            ref[:, pl.ds(row, SUBS), :] = jnp.zeros((nh, SUBS, LANES), F32)
    edge_c, edge_r = (me_c == 0, me_c == ncols - 1), (me_r == 0, me_r == nrows - 1)
    for side in range(2):
        @pl.when(edge_c[side])
        def _(side=side):
            for ref in (gyk.at[side], gyu.at[side], gyw.at[0, side], gyw.at[1, side],
                        gyp.at[0, side], gyp.at[1, side]):
                ref[...] = jnp.zeros(ref.shape, F32)

        @pl.when(edge_r[side])
        def _(side=side):
            for ref in (gxk.at[side], gxu.at[side], gxw.at[0, side], gxw.at[1, side],
                        gxp.at[0, side], gxp.at[1, side]):
                ref[...] = jnp.zeros(ref.shape, F32)
        for other in range(2):
            @pl.when(jnp.logical_or(edge_r[side], edge_c[other]))
            def _(q=2 * side + other):
                for ref in (gck.at[q], gcw.at[0, q], gcw.at[1, q]):
                    ref[...] = jnp.zeros(ref.shape, F32)

    sent = []

    def transfer(src, dst, dr, dc):
        def exists(step_r, step_c):
            tests = []
            if step_r:
                tests.append(me_r < nrows - 1 if step_r > 0 else me_r > 0)
            if step_c:
                tests.append(me_c < ncols - 1 if step_c > 0 else me_c > 0)
            return functools.reduce(jnp.logical_and, tests)
        n = len(sent)
        copy = pltpu.make_async_remote_copy(
            src_ref=src, dst_ref=dst, send_sem=hs_sem.at[n], recv_sem=hr_sem.at[n],
            device_id=(me_r + dr, me_c + dc), device_id_type=MESH)
        has_target = exists(dr, dc)
        sent.append((has_target, copy))

        @pl.when(has_target)
        def _():
            copy.start()
        return exists(-dr, -dc), copy

    def arrive(copies):
        for has_source, copy in copies:
            @pl.when(has_source)
            def _(copy=copy):
                copy.wait_recv()

    def toward(side):
        return 1 if side == 0 else -1

    def strided(side, depth=0):
        return pl.ds(OFF + (depth if side == 0 else ny - 1 - depth), nx, stride=ny)

    def plane_at(side, depth=0):
        return pl.ds(OFF + (depth if side == 0 else nx - 1 - depth) * ny, ny)

    def corner_at(q):
        return pl.ds(OFF + (q // 2) * (nx - 1) * ny + (q % 2) * (ny - 1), 1)

    along = pl.ds(SUBS, nx)
    across = pl.ds(SUBS, ny)

    def send_corners(ref, mine, theirs):
        made = []
        for q in range(4):
            mine[q] = ref[:, corner_at(q), :]
        for q in range(4):
            made.append(transfer(mine.at[3 - q], theirs.at[q], toward(q // 2), toward(q % 2)))
        return made

    for cp in loads[:2 * nh]:
        cp.wait()
    for side in range(2):
        for h in halves:
            fyk[side, h] = kk[h, strided(side), :]
            fyu[side, h] = uu[h, strided(side), :]
    pl.semaphore_wait(barrier, len(greeted))
    first = []
    for side in range(2):
        t = toward(side)
        first.append(transfer(fyk.at[1 - side], gyk.at[side], 0, t))
        first.append(transfer(fyu.at[1 - side], gyu.at[side], 0, t))
    for side in range(2):
        t = toward(side)
        first.append(transfer(kk.at[:, plane_at(1 - side), :], gxk.at[side], t, 0))
        first.append(transfer(uu.at[:, plane_at(1 - side), :], gxu.at[side], t, 0))
    second = send_corners(kk, ck, gck)
    if one_stage:
        for dr, dc in row_peers:
            pl.semaphore_signal(in_sem, inc=1, device_id_type=MESH, device_id=device(dr, dc))

    lane = lax.broadcasted_iota(jnp.int32, (SUBS, LANES), 1)
    sub = lax.broadcasted_iota(jnp.int32, (SUBS, LANES), 0)
    first_lane, last_lane = lane == 0, lane == LANES - 1
    first_sub, last_sub = sub == 0, sub == SUBS - 1
    zero = jnp.zeros((SUBS, LANES), F32)
    sixteenth = 0.5 / SCALE

    def tile(ref, h, g, base, offset=0):
        return ref[h, pl.ds(base + (g * SUBS + offset), SUBS), :]

    def get(ref, base, offset=0):
        return {(h, g): tile(ref, h, g, base, offset) for h, g in cells}

    def put(ref, base, values):
        for h, g in cells:
            ref[h, pl.ds(base + g * SUBS, SUBS), :] = values[h, g]

    def y_down(v):
        r = {c: pltpu.roll(v[c], 1, 0) for c in cells}
        return {(h, g): jnp.where(first_sub, r[h, g - 1], r[h, g]) if g > 0 else r[h, g]
                for h, g in cells}

    def z_up(v):
        r = {c: pltpu.roll(v[c], LANES - 1, 1) for c in v}
        return {(h, g): jnp.where(last_lane, r[h + 1, g], r[h, g]) if h < nh - 1 else r[h, g]
                for h, g in v}

    def z_down(v):
        r = {c: pltpu.roll(v[c], 1, 1) for c in v}
        return {(h, g): jnp.where(first_lane, r[h - 1, g], r[h, g]) if h > 0 else r[h, g]
                for h, g in v}

    flat = lambda v: tuple(v[c] for c in cells)
    dict_of = lambda t: dict(zip(cells, t))

    def coef_body(i, carry):
        here, cx_before = dict_of(carry[0]), dict_of(carry[1])
        for q in range(PLANES):
            low = pl.multiple_of((i * PLANES + q) * ny, ny)
            base = low + OFF
            after = get(kk, base + ny)
            up, right = get(kk, base, 1), z_up(here)
            fx = {c: (here[c] + after[c]) * sixteenth for c in cells}
            fy_ = {c: (here[c] + up[c]) * sixteenth for c in cells}
            fz = {c: (here[c] + right[c]) * sixteenth for c in cells}
            for h in halves:
                fy_[h, ng - 1] = jnp.where(last_sub, 0.0, fy_[h, ng - 1])
            for g in range(ng):
                fz[nh - 1, g] = jnp.where(last_lane, 0.0, fz[nh - 1, g])
            fyb, fzb = y_down(fy_), z_down(fz)
            for h in halves:
                fyb[h, 0] = jnp.where(first_sub, 0.0, fyb[h, 0])
            for g in range(ng):
                fzb[0, g] = jnp.where(first_lane, 0.0, fzb[0, g])
            total = {c: ((fx[c] + cx_before[c]) + (fy_[c] + fyb[c])) + (fz[c] + fzb[c])
                     for c in cells}
            for g in range(ng):
                total[0, g] = total[0, g] + jnp.where(first_lane, here[0, g] * sixteenth, 0.0)
                total[nh - 1, g] = total[nh - 1, g] + jnp.where(
                    last_lane, here[nh - 1, g] * sixteenth, 0.0)
            for ref, val in ((cx, fx), (cy, fy_), (cyb, fyb), (cz, fz), (czb, fzb), (diag, total)):
                put(ref, base, val)
            here, cx_before = after, fx
        return flat(here), flat(cx_before)

    lax.fori_loop(0, nx // PLANES, coef_body, (flat(get(kk, OFF)), (zero,) * len(cells)))
    last = OFF + count - ny
    put(diag, last, {c: tile(diag, *c, last) - tile(cx, *c, last) for c in cells})
    put(cx, last, {c: zero for c in cells})

    rows_in = [jnp.where((sub + g * SUBS >= 2) & (sub + g * SUBS < ny - 2), 1.0, 0.0).astype(F32)
               for g in range(ng)]

    def stencil(src, dst, shift, residual, pairs):
        def body(i, carry):
            here, before, cx_before = (dict_of(t) for t in carry[:3])
            accs = [list(t) for t in carry[3]]
            ends = {}
            if any(masked for _, _, masked in pairs):
                low_on = jnp.where(i > 0, 1.0, 0.0).astype(F32)
                high_on = jnp.where(i < nx // PLANES - 1, 1.0, 0.0).astype(F32)
                for q in (0, 1):
                    ends[q] = [m * low_on for m in rows_in]
                    ends[PLANES - 1 - q] = [m * high_on for m in rows_in]
            for q in range(PLANES):
                low = pl.multiple_of((i * PLANES + q) * ny, ny)
                base = low + OFF
                after = get(src, base + ny)
                up, down, right, left = get(src, base, 1), get(src, base, -1), z_up(here), z_down(here)
                new = {}
                fx = get(cx, base)
                for c in cells:
                    d = tile(diag, *c, base)
                    val = (d - shift if shift else d) * here[c]
                    val = val - fx[c] * after[c]
                    val = val - cx_before[c] * before[c]
                    val = val - tile(cy, *c, base) * up[c]
                    val = val - tile(cyb, *c, base) * down[c]
                    val = val - tile(cz, *c, base) * right[c]
                    val = val - tile(czb, *c, base) * left[c]
                    if residual:
                        val = tile(rs, *c, low) - SCALE * val
                    new[c] = val
                put(dst, base, new)
                known = {"here": here, "new": new}
                for h, g in cells:
                    mask = ends.get(q, rows_in)[g]
                    inside = {}
                    for acc, (one, two, masked) in zip(accs, pairs):
                        first_of, second_of = (
                            known[v][h, g] if isinstance(v, str) else tile(v, h, g, base)
                            for v in (one, two))
                        if masked:
                            if one not in inside:
                                inside[one] = first_of * mask
                            first_of = inside[one]
                        acc[h] = acc[h] + first_of * second_of
                before, here, cx_before = here, after, fx
            return flat(here), flat(before), flat(cx_before), tuple(tuple(a) for a in accs)
        nothing = (zero,) * len(cells)
        out = lax.fori_loop(0, nx // PLANES, body,
                            (flat(get(src, OFF)), nothing, nothing, ((zero,) * nh,) * len(pairs)))
        return [add_up(list(t)) for t in out[3]]

    for cp in loads[2 * nh:]:
        cp.wait()
    stencil(uu, w[0], 0.0, True, [])
    for side in range(2):
        for h in halves:
            for e, ref in ((3, cz), (4, czb), (5, cyb if side else cy), (1, cx)):
                own_y[side, e, h] = ref[h, strided(side), :]
            bump_y[h, along, :] = own_y[side, 1, h]
        for h in halves:
            own_y[side, 2, h] = bump_y[h, pl.ds(SUBS - 1, nx), :]
    arrive(first)
    for side in range(2):
        at = plane_at(side)
        coef = (kk[:, at, :] + gxk[side]) * sixteenth
        cfx[side] = coef
        w[0][:, at, :] = w[0][:, at, :] - SCALE * (coef * (uu[:, at, :] - gxu[side]))
    for side in range(2):
        for h in halves:
            coef = (fyk[side, h] + gyk[side, h]) * sixteenth
            cfy[side, h] = coef
            fyw[0, side, h] = w[0][h, strided(side), :] - SCALE * (
                coef * (fyu[side, h] - gyu[side, h]))

    def send_near(r, ref):
        made = []
        for side in range(2):
            made.append(transfer(fyw.at[r, 1 - side], gyw.at[r, side], 0, toward(side)))
        for side in range(2):
            for h in halves:
                ref[h, strided(side), :] = fyw[r, side, h]
        for side in range(2):
            made.append(transfer(ref.at[:, plane_at(1 - side), :], gxw.at[r, side], toward(side), 0))
        return made, send_corners(ref, cw.at[r], gcw.at[r])

    def sideways(values, step):
        length = values[0].shape[0]
        index = lax.broadcasted_iota(jnp.int32, (length, LANES), 1)
        rolled = [pltpu.roll(v, LANES - 1 if step > 0 else 1, 1) for v in values]
        made = []
        for h in halves:
            if step > 0 and h < nh - 1:
                made.append(jnp.where(index == LANES - 1, rolled[h + 1], rolled[h]))
            elif step < 0 and h > 0:
                made.append(jnp.where(index == 0, rolled[h - 1], rolled[h]))
            else:
                made.append(rolled[h])
        return made

    def shifted_rows(ref, length, step):
        return [ref[h, pl.ds(SUBS + step, length), :] for h in halves]

    def in_plane(values, inside, shift, bump, length):
        for h in halves:
            bump[h, pl.ds(SUBS, length), :] = values[h]
        right, left = sideways(values, 1), sideways(values, -1)
        up, down = shifted_rows(bump, length, 1), shifted_rows(bump, length, -1)
        made = []
        for h in halves:
            total, fu, fd, fz, fzb = (inside(e, h) for e in range(5))
            val = (total - shift) * values[h] - fu * up[h] - fd * down[h]
            made.append(val - fz * right[h] - fzb * left[h])
        return made

    def x_coefs(side):
        at = plane_at(side)
        def inside(e, h):
            if e == 5:
                return cx[h, plane_at(side, 0 if side == 0 else 1), :]
            return (diag, cy, cyb, cz, czb)[e][h, at, :]
        return inside

    def y_coefs(side):
        return lambda e, h: own_y[side, e, h]

    there_c = [jnp.where(e, 0.0, 1.0).astype(F32) for e in edge_c]
    there_r = [jnp.where(e, 0.0, 1.0).astype(F32) for e in edge_r]

    def send_next(r, src, shift):
        made = []
        for side in range(2):
            within = [src[h, strided(side, 1), :] for h in halves]
            val = in_plane([fyw[r, side, h] for h in halves], y_coefs(side), shift, bump_y, nx)
            for h in halves:
                fyp[r, side, h] = val[h] - own_y[side, 5, h] * within[h]
                if r:
                    inner_y[side, h] = within[h]
        for side in range(2):
            made.append(transfer(fyp.at[r, 1 - side], gyp.at[r, side], 0, toward(side)))
        for side in range(2):
            at, below = plane_at(side), plane_at(side, 1)
            inside = x_coefs(side)
            val = in_plane([src[h, at, :] for h in halves], inside, shift, bump_x, ny)
            for h in halves:
                fxp[r, side, h] = val[h] - inside(5, h) * src[h, below, :]
        for side in range(2):
            made.append(transfer(fxp.at[r, 1 - side], gxp.at[r, side], toward(side), 0))
        return made

    def mend(mid, r):
        for side in range(2):
            at = plane_at(side)
            for h in halves:
                mid[h, at, :] = mid[h, at, :] + gxw[r, side, h]
        for side in range(2):
            for h in halves:
                new = mid[h, strided(side), :] + gyw[r, side, h]
                mid[h, strided(side), :] = new
                if r:
                    gyw[r, side, h] = new

    sums = {}
    for r in range(2):
        src, mid, dst = w[2 * r:2 * r + 3]
        shift_one, shift_two = NEWTON[2 * r] / SCALE, NEWTON[2 * r + 1] / SCALE
        near, corners = send_near(r, src)
        if r == 0:
            for side in range(2):
                at = plane_at(side)
                diag[:, at, :] = diag[:, at, :] + cfx[side]
            for side in range(2):
                for h in halves:
                    own_y[side, 0, h] = diag[h, strided(side), :] + cfy[side, h]
                    diag[h, strided(side), :] = own_y[side, 0, h]
        far = send_next(r, src, shift_one)
        if r == 0:
            sums[0, 0], = stencil(src, mid, shift_one, False, [("here", "here", False)])
            stencil(mid, dst, shift_two, False, [])
            arrive(second)
            for side in range(2):
                for end in range(2):
                    q = 2 * end + side
                    corner_y[side, end] = (gck[q] + gyk[side, :, pl.ds(end * (nx - 1), 1), :]) * sixteenth
                    q = 2 * side + end
                    corner_x[side, end] = (gck[q] + gxk[side, :, pl.ds(end * (ny - 1), 1), :]) * sixteenth
        else:
            mend(w[1], 0)
            sums[2, 2], sums[1, 2], sums[1, 1], sums[0, 1] = stencil(
                src, mid, shift_one, False,
                [("here", "here", False), ("here", w[1], False), (w[1], w[1], False),
                 (w[1], w[0], False)])
            last_four = stencil(
                mid, dst, shift_two, False,
                [("here", "here", True), ("here", w[2], True), ("new", "new", True),
                 ("new", "here", True)])
        near_y, near_x, far_y, far_x = near[:2], near[2:], far[:2], far[2:]
        arrive(near_x)
        arrive(far_x)
        arrive(corners)
        for side in range(2):
            at, below = plane_at(side), plane_at(side, 1)
            inside = x_coefs(side)
            one = [-(cfx[side, h] * gxw[r, side, h]) for h in halves]
            two = in_plane(one, inside, shift_two, bump_x, ny)
            for end in range(2):
                row_at = pl.ds(end * (ny - 1), 1)
                gxp[r, side, :, row_at, :] = (
                    gxp[r, side, :, row_at, :] - corner_x[side, end] * gcw[r, 2 * side + end])
            for h in halves:
                gxw[r, side, h] = one[h]
                val = (gxp[r, side, h] - cfx[side, h] * src[h, at, :]) * there_r[side]
                dst[h, at, :] = dst[h, at, :] + (two[h] - cfx[side, h] * val)
                dst[h, below, :] = dst[h, below, :] - inside(5, h) * one[h]
        arrive(near_y)
        for side in range(2):
            one = [-(cfy[side, h] * gyw[r, side, h]) for h in halves]
            two = in_plane(one, y_coefs(side), shift_two, bump_y, nx)
            for h in halves:
                two_y[side, h] = cfy[side, h] * fyw[r, side, h]
            for end in range(2):
                row_at = pl.ds(end * (nx - 1), 1)
                two_y[side, :, row_at, :] = (
                    two_y[side, :, row_at, :] + corner_y[side, end] * gcw[r, 2 * end + side])
            for h in halves:
                gyw[r, side, h] = one[h]
                weight = cfy[side, h] * there_c[side]
                outer_y[side, h] = dst[h, strided(side), :] + (two[h] + weight * two_y[side, h])
                within = dst[h, strided(side, 1), :] - own_y[side, 5, h] * one[h]
                dst[h, strided(side, 1), :] = within
                two_y[side, h] = within
        arrive(far_y)
        for side in range(2):
            for h in halves:
                outer = outer_y[side, h] - (cfy[side, h] * there_c[side]) * gyp[r, side, h]
                if r == 0:
                    fyw[1, side, h] = outer
                else:
                    dst[h, strided(side), :] = outer
                    outer_y[side, h] = outer
    mend(w[3], 1)

    def fold(values):
        return jnp.sum(values.reshape(-1, SUBS, LANES), axis=0)

    row = lax.broadcasted_iota(jnp.int32, (nx, LANES), 0)
    planes_in = (row >= 2) & (row < nx - 2)
    for side in range(2):
        for h in halves:
            for two_at, three_at, four_at in (
                    (fyw[1, side, h], gyw[1, side, h], outer_y[side, h]),
                    (inner_y[side, h], w[3][h, strided(side, 1), :], two_y[side, h])):
                third = jnp.where(planes_in, three_at, 0.0)
                fourth = jnp.where(planes_in, four_at, 0.0)
                for e, val in enumerate((third * three_at, third * two_at,
                                         fourth * four_at, fourth * three_at)):
                    last_four[e] = last_four[e] + fold(val)
            for depth in range(2):
                at = plane_at(side, depth)
                two_at, three_at, four_at = (w[k][h, at, :] for k in (2, 3, 4))
                for e, val in enumerate((three_at * three_at, three_at * two_at,
                                         four_at * four_at, four_at * three_at)):
                    last_four[e] = last_four[e] + fold(val)
    sums[3, 3], sums[2, 3], sums[4, 4], sums[3, 4] = last_four


    def exchange(buf, ssem, rsem, peers, value):
        here = len(peers)
        buf[here] = value
        for e, (dr, dc) in enumerate(peers):
            pltpu.make_async_remote_copy(
                src_ref=buf.at[here], dst_ref=buf.at[e], send_sem=ssem.at[0], recv_sem=rsem.at[0],
                device_id=device(dr, dc), device_id_type=MESH).start()
        whole = buf.at[pl.ds(0, here)]
        pltpu.make_async_copy(whole, whole, rsem.at[0]).wait()
        parts = [buf[i] for i in range(here + 1)]
        while len(parts) > 1:
            parts = [a + b for a, b in zip(parts[::2], parts[1::2])] + (
                parts[-1:] if len(parts) % 2 else [])
        return parts[0]

    def finish_sends(buf, ssem, peers):
        whole = buf.at[pl.ds(0, len(peers))]
        pltpu.make_async_copy(whole, whole, ssem.at[0]).wait()

    everyone = [(dr, dc) for dr in range(nrows) for dc in range(ncols)][1:]
    pair_row = lax.broadcasted_iota(jnp.int32, (16, LANES), 0)
    on_diag = pair_row == lax.broadcasted_iota(jnp.int32, (16, LANES), 1)
    gm[...] = jnp.zeros(gm.shape, F32)
    for e, pair in enumerate(SUMS):
        gm[e:e + 1, :] = jnp.sum(sums[pair], axis=0, keepdims=True)
    line = jnp.sum(jnp.where(on_diag, jnp.sum(gm[...], axis=1, keepdims=True), 0.0),
                   axis=0, keepdims=True)
    if one_stage:
        pl.semaphore_wait(in_sem, len(row_peers))
        line = exchange(g1, s1, r1, everyone, line)
    else:
        line = exchange(g1, s1, r1, col_peers, line)
        line = exchange(g2, s2, r2, row_peers, line)
    gm[...] = jnp.broadcast_to(
        jnp.sum(jnp.where(on_diag, line, 0.0), axis=1, keepdims=True), gm.shape)
    moments = {pair: gm[e:e + 1, :] for e, pair in enumerate(SUMS)}
    for gap in range(2, 5):
        for i in range(5 - gap):
            j = i + gap
            moments[i, j] = moments[i + 1, j - 1] + (
                (NEWTON[i] - NEWTON[j - 1]) / SCALE) * moments[i, j - 1]
            moments[i, j] = moments[i, j]
    gram_one = lambda i, j: moments[min(i, j), max(i, j)]
    low_one, inv_one = cholesky(gram_one, 5)
    linv_one = lower_inverse(low_one, inv_one, 5)
    half = {(i, j): add_up([linv_one[i, m] * gram_one(m, j) for m in range(i + 1)])
            for i in range(5) for j in range(i + 1)}
    gram_two = {(i, j): add_up([half[i, m] * linv_one[j, m] for m in range(j + 1)])
                for i in range(5) for j in range(i + 1)}
    low_two, inv_two = cholesky(lambda i, j: gram_two[i, j], 5)
    linv_two = lower_inverse(low_two, inv_two, 5)

    trans = {(i, j): add_up([linv_two[i, m] * linv_one[m, j] for m in range(j, i + 1)])
             for i in range(5) for j in range(i + 1)}
    rfac = {(i, j): add_up([low_two[m, i] * low_one[j, m] for m in range(i, j + 1)])
            for i in range(5) for j in range(i, 5)}
    shifted = {}
    for k in range(4):
        for i in range(k + 2):
            val = rfac[i, k + 1] * SCALE
            shifted[i, k] = val + rfac[i, k] * NEWTON[k] if i <= k else val
    hess = {(i, k): add_up([shifted[i, m] * trans[k, m] for m in range(max(i - 1, 0), k + 1)])
            for k in range(4) for i in range(k + 2)}
    target, inv_n = [rfac[0, 0]], []
    for k in range(4):
        top, bottom = hess[k, k], hess[k + 1, k]
        square = top * top + bottom * bottom
        inv_n.append(inv_sqrt(square))
        cosine, sine = top * inv_n[k], bottom * inv_n[k]
        for j in range(k + 1, 4):
            upper, under = hess[k, j], hess[k + 1, j]
            hess[k, j] = cosine * upper + sine * under
            hess[k + 1, j] = cosine * under - sine * upper
        target.append(-(sine * target[k]))
        target[k] = cosine * target[k]
    weights = [None] * 4
    for i in range(3, -1, -1):
        val = target[i]
        for m in range(i + 1, 4):
            val = val - hess[i, m] * weights[m]
        weights[i] = val * inv_n[i]

    root = math.sqrt(nrows * ncols * nx * ny * nz)
    for e, (j, i) in enumerate(PAIRS):
        coef_out[e:e + 1, :] = trans[i, j] * root
    for k in range(4):
        coef_out[16 + k:17 + k, :] = weights[k] * (1.0 / root)
    one_row = lax.broadcasted_iota(jnp.int32, (1, LANES), 1)
    for i in range(5):
        line = jnp.zeros((1, LANES), F32)
        column = [rfac[i, 0] if i == 0 else jnp.zeros((1, LANES), F32)]
        for j in range(1, 5):
            below = rfac[i, j] if j >= i else 0.0
            column.append(below - column[j - 1] * (SHIFTS[j - 1] / SCALE))
        for j in range(i, 5):
            line = jnp.where(one_row == j, column[j], line)
        coef_out[24 + i:25 + i, :] = line

    if one_stage:
        finish_sends(g1, s1, everyone)
    else:
        finish_sends(g1, s1, col_peers)
        finish_sends(g2, s2, row_peers)
    for has_target, copy in sent:
        @pl.when(has_target)
        def _(copy=copy):
            copy.wait_send()


def finish_kernel(parts, nz, w_ref, coef_ref, basis_hbm, rfac_ref, updated_hbm, stage, last, sems):
    trans = {(i, j): jnp.broadcast_to(coef_ref[e:e + 1, :], (SUBS, LANES))
             for e, (j, i) in enumerate(PAIRS)}
    weights = [jnp.broadcast_to(coef_ref[16 + k:17 + k, :], (SUBS, LANES)) for k in range(4)]
    rfac_ref[...] = coef_ref[24:29, 0:5]
    copies = []
    for part, (start, size) in enumerate(parts):

        def body(n, carry):
            low = pl.multiple_of(start + n * SUBS, SUBS)
            at, rows_in = pl.ds(low, SUBS), pl.ds(low + OFF, SUBS)
            for h in range(nz // LANES):
                lanes = pl.ds(h * LANES, LANES)
                raw = [w_ref[k, h, rows_in, :] for k in range(5)]
                new = w_ref[5, h, rows_in, :]
                for i in range(5):
                    val = trans[i, 0] * raw[0]
                    for j in range(1, i + 1):
                        val = val + trans[i, j] * raw[j]
                    stage[i, at, lanes] = val
                    if i < 4:
                        new = new + weights[i] * val
                last[at, lanes] = new
            return carry
        lax.fori_loop(0, size // SUBS, body, 0, unroll=8)
        rows = pl.ds(start, size)
        for e, (src, dst) in enumerate(((stage.at[:, rows, :], basis_hbm.at[:, rows, :]),
                                        (last.at[rows, :], updated_hbm.at[rows, :]))):
            copies.append(pltpu.make_async_copy(src, dst, sems.at[part, e]))
            copies[-1].start()
    for copy in copies:
        copy.wait()


def on_device(nrows, ncols, right_side, initial, conduct):
    nx, ny, nz = initial.shape
    nh, count = nz // LANES, nx * ny
    flat = [a.reshape(count, nz) for a in (right_side, initial, conduct)]
    dma = pltpu.SemaphoreType.DMA
    slots = nrows * ncols if nrows * ncols <= 64 else ncols
    field = pltpu.VMEM((nh, count, LANES), F32)
    padded = pltpu.VMEM((nh, OFF + count + ny, LANES), F32)
    ends = 2 * SUBS
    y_pair, x_pair = pltpu.VMEM((2, nh, nx, LANES), F32), pltpu.VMEM((2, nh, ny, LANES), F32)
    y_four, x_four = pltpu.VMEM((2, 2, nh, nx, LANES), F32), pltpu.VMEM((2, 2, nh, ny, LANES), F32)
    vectors, coefs = pl.pallas_call(
        functools.partial(cycle_kernel, (nrows, ncols, nx, ny, nz)),
        out_shape=(pltpu.VMEM((6, nh, OFF + count + ny, LANES), F32),
                   pltpu.VMEM((32, LANES), F32)),
        in_specs=[pl.BlockSpec(memory_space=pltpu.HBM)] * 3,
        out_specs=(pl.BlockSpec(memory_space=pltpu.VMEM), pl.BlockSpec(memory_space=pltpu.VMEM)),
        scratch_shapes=[
            padded, field, padded, padded, padded, padded, padded, padded,
            pltpu.VMEM((2, nh, ny, LANES), F32), pltpu.VMEM((2, nh, nx, LANES), F32),
            y_pair, y_pair, y_four, y_four, x_four, y_pair, y_pair, y_four, y_four,
            x_pair, x_pair, x_four, x_four,
            pltpu.VMEM((4, nh, 1, LANES), F32), pltpu.VMEM((2, 4, nh, 1, LANES), F32),
            pltpu.VMEM((4, nh, 1, LANES), F32), pltpu.VMEM((2, 4, nh, 1, LANES), F32),
            pltpu.VMEM((2, 2, nh, 1, LANES), F32), pltpu.VMEM((2, 2, nh, 1, LANES), F32),
            pltpu.VMEM((2, 6, nh, nx, LANES), F32), y_pair, y_pair, y_pair,
            pltpu.VMEM((nh, nx + ends, LANES), F32), pltpu.VMEM((nh, ny + ends, LANES), F32),
            pltpu.VMEM((slots, 1, LANES), F32), pltpu.VMEM((nrows, 1, LANES), F32),
            pltpu.VMEM((16, LANES), F32),
            dma((3, nh)), dma((36,)), dma((36,)),
            dma((1,)), dma((1,)), dma((1,)), dma((1,)), pltpu.SemaphoreType.REGULAR,
        ],
        compiler_params=pltpu.CompilerParams(
            collective_id=0, has_side_effects=True, vmem_limit_bytes=57 << 20),
        name="cycle",
    )(*flat)
    unit = count // 16
    sizes = [unit * n for n in (1, 3, 4, 4, 3, 1)]
    parts = [(sum(sizes[:i]), size) for i, size in enumerate(sizes)]
    basis, rfactor, updated = pl.pallas_call(
        functools.partial(finish_kernel, parts, nz),
        out_shape=(jax.ShapeDtypeStruct((5, count, nz), F32),
                   jax.ShapeDtypeStruct((5, 5), F32),
                   jax.ShapeDtypeStruct((count, nz), F32)),
        in_specs=[pl.BlockSpec(memory_space=pltpu.VMEM)] * 2,
        out_specs=(pl.BlockSpec(memory_space=pltpu.HBM), pl.BlockSpec(memory_space=pltpu.VMEM),
                   pl.BlockSpec(memory_space=pltpu.HBM)),
        scratch_shapes=[pltpu.VMEM((5, count, nz), F32), pltpu.VMEM((count, nz), F32),
                        dma((len(parts), 2))],
        compiler_params=pltpu.CompilerParams(vmem_limit_bytes=20 << 20),
        name="finish",
    )(vectors, coefs)
    return (basis.reshape(5, nx, ny, nz), rfactor, updated.reshape(nx, ny, nz))


def solution(mesh):
    nrows, ncols = mesh.shape["rows"], mesh.shape["cols"]
    return jax.shard_map(
        functools.partial(on_device, nrows, ncols),
        mesh=mesh,
        in_specs=(P("rows", "cols", None),) * 3,
        out_specs=(P(None, "rows", "cols", None), P(), P("rows", "cols", None)),
        check_vma=False,
    )
```

```python
import functools
import math

import jax
import jax.numpy as jnp
from jax import lax
from jax.experimental import pallas as pl
from jax.experimental.pallas import tpu as pltpu
from jax.sharding import PartitionSpec as P

SHIFTS = (12.0, 3.0, 21.0, 7.0)
NEWTON = (0.0,) + SHIFTS[:3]
SCALE = 8.0
LANES = 128
SUBS = 8
PLANES = 8
OFF = SUBS
MESH = pl.DeviceIdType.MESH
PAIRS = [(i, j) for j in range(5) for i in range(j + 1)]
SUMS = [(0, 0)] + [(k - d, k) for k in range(1, 5) for d in (1, 0)]
F32 = jnp.float32


def inv_sqrt(value):
    guess = lax.rsqrt(value)
    return guess * (1.5 - 0.5 * (value * guess) * guess)


def cholesky(entry, order):
    lower, inv = {}, []
    for col in range(order):
        diag = entry(col, col)
        for inner in range(col):
            diag = diag - lower[col, inner] * lower[col, inner]
        root = inv_sqrt(diag)
        inv.append(root)
        lower[col, col] = diag * root
        for row in range(col + 1, order):
            val = entry(row, col)
            for inner in range(col):
                val = val - lower[row, inner] * lower[col, inner]
            lower[row, col] = val * root
    return lower, inv


def lower_inverse(lower, inv, order):
    result = {}
    for row in range(order):
        for col in range(row):
            total = lower[row, col] * result[col, col]
            for inner in range(col + 1, row):
                total = total + lower[row, inner] * result[inner, col]
            result[row, col] = -(total * inv[row])
        result[row, row] = inv[row]
    return result


def add_up(terms):
    return functools.reduce(lambda a, b: a + b, terms)


def cycle_kernel(sizes, rs_hbm, init_hbm, cond_hbm, w_out, coef_out,
                 kk, rs, diag, cx, cy, cyb, cz, czb, cfx, cfy,
                 fyk, fyu, fyw, fyp, fxp, gyk, gyu, gyw, gyp, gxk, gxu, gxw, gxp, ck, cw, gck, gcw,
                 corner_y, corner_x, own_y, two_y, inner_y, outer_y, bump_y, bump_x,
                 g1, g2, gm, load_sem, hs_sem, hr_sem, s1, r1, s2, r2, in_sem):
    nrows, ncols, nx, ny, nz = sizes
    nh, ng = nz // LANES, ny // SUBS
    count = nx * ny
    one_stage = nrows * ncols <= 64
    halves = range(nh)
    cells = [(h, g) for h in halves for g in range(ng)]
    me_r, me_c = lax.axis_index("rows"), lax.axis_index("cols")
    uu = w_out.at[5]
    w = [w_out.at[k] for k in range(5)]
    inner = pl.ds(OFF, count)

    barrier = pltpu.get_barrier_semaphore()
    col_peers = [(0, d) for d in range(1, ncols)]
    row_peers = [(d, 0) for d in range(1, nrows)]
    greeted = col_peers + row_peers + sorted(
        {(dr % nrows, dc % ncols) for dr in (-1, 1) for dc in (-1, 1)}
        - set(col_peers + row_peers + [(0, 0)]))

    def device(dr, dc):
        return (lax.rem(me_r + dr, nrows), lax.rem(me_c + dc, ncols))

    for dr, dc in greeted:
        pl.semaphore_signal(barrier, inc=1, device_id_type=MESH, device_id=device(dr, dc))

    loads = []
    for idx, (src, dst) in enumerate(((cond_hbm, kk), (init_hbm, uu), (rs_hbm, rs))):
        for h in halves:
            loads.append(pltpu.make_async_copy(
                src.at[:, pl.ds(h * LANES, LANES)],
                dst.at[h, inner if idx < 2 else pl.ds(0, count), :], load_sem.at[idx, h]))
            loads[-1].start()

    for ref in [kk] + [w_out.at[i] for i in range(6)]:
        ref[:, pl.ds(0, OFF), :] = jnp.zeros((nh, OFF, LANES), F32)
        ref[:, pl.ds(OFF + count, ny), :] = jnp.zeros((nh, ny, LANES), F32)
    for ref, length in ((bump_y, nx), (bump_x, ny)):
        for row in (0, SUBS + length):
            ref[:, pl.ds(row, SUBS), :] = jnp.zeros((nh, SUBS, LANES), F32)
    edge_c, edge_r = (me_c == 0, me_c == ncols - 1), (me_r == 0, me_r == nrows - 1)
    for side in range(2):
        @pl.when(edge_c[side])
        def _(side=side):
            for ref in (gyk.at[side], gyu.at[side], gyw.at[0, side], gyw.at[1, side],
                        gyp.at[0, side], gyp.at[1, side]):
                ref[...] = jnp.zeros(ref.shape, F32)

        @pl.when(edge_r[side])
        def _(side=side):
            for ref in (gxk.at[side], gxu.at[side], gxw.at[0, side], gxw.at[1, side],
                        gxp.at[0, side], gxp.at[1, side]):
                ref[...] = jnp.zeros(ref.shape, F32)
        for other in range(2):
            @pl.when(jnp.logical_or(edge_r[side], edge_c[other]))
            def _(q=2 * side + other):
                for ref in (gck.at[q], gcw.at[0, q], gcw.at[1, q]):
                    ref[...] = jnp.zeros(ref.shape, F32)

    sent = []

    def transfer(src, dst, dr, dc):
        def exists(step_r, step_c):
            tests = []
            if step_r:
                tests.append(me_r < nrows - 1 if step_r > 0 else me_r > 0)
            if step_c:
                tests.append(me_c < ncols - 1 if step_c > 0 else me_c > 0)
            return functools.reduce(jnp.logical_and, tests)
        n = len(sent)
        copy = pltpu.make_async_remote_copy(
            src_ref=src, dst_ref=dst, send_sem=hs_sem.at[n], recv_sem=hr_sem.at[n],
            device_id=(me_r + dr, me_c + dc), device_id_type=MESH)
        has_target = exists(dr, dc)
        sent.append((has_target, copy))

        @pl.when(has_target)
        def _():
            copy.start()
        return exists(-dr, -dc), copy

    def arrive(copies):
        for has_source, copy in copies:
            @pl.when(has_source)
            def _(copy=copy):
                copy.wait_recv()

    def toward(side):
        return 1 if side == 0 else -1

    def strided(side, depth=0):
        return pl.ds(OFF + (depth if side == 0 else ny - 1 - depth), nx, stride=ny)

    def plane_at(side, depth=0):
        return pl.ds(OFF + (depth if side == 0 else nx - 1 - depth) * ny, ny)

    def corner_at(q):
        return pl.ds(OFF + (q // 2) * (nx - 1) * ny + (q % 2) * (ny - 1), 1)

    along = pl.ds(SUBS, nx)
    across = pl.ds(SUBS, ny)

    def send_corners(ref, mine, theirs):
        made = []
        for q in range(4):
            mine[q] = ref[:, corner_at(q), :]
        for q in range(4):
            made.append(transfer(mine.at[3 - q], theirs.at[q], toward(q // 2), toward(q % 2)))
        return made

    for cp in loads[:2 * nh]:
        cp.wait()
    for side in range(2):
        for h in halves:
            fyk[side, h] = kk[h, strided(side), :]
            fyu[side, h] = uu[h, strided(side), :]
    pl.semaphore_wait(barrier, len(greeted))
    first = []
    for side in range(2):
        first.append(transfer(fyk.at[1 - side], gyk.at[side], 0, toward(side)))
    for side in range(2):
        first.append(transfer(fyu.at[1 - side], gyu.at[side], 0, toward(side)))
    for side in range(2):
        t = toward(side)
        first.append(transfer(kk.at[:, plane_at(1 - side), :], gxk.at[side], t, 0))
        first.append(transfer(uu.at[:, plane_at(1 - side), :], gxu.at[side], t, 0))
    second = send_corners(kk, ck, gck)
    if one_stage:
        for dr, dc in row_peers:
            pl.semaphore_signal(in_sem, inc=1, device_id_type=MESH, device_id=device(dr, dc))

    lane = lax.broadcasted_iota(jnp.int32, (SUBS, LANES), 1)
    sub = lax.broadcasted_iota(jnp.int32, (SUBS, LANES), 0)
    first_lane, last_lane = lane == 0, lane == LANES - 1
    first_sub, last_sub = sub == 0, sub == SUBS - 1
    zero = jnp.zeros((SUBS, LANES), F32)
    sixteenth = 0.5 / SCALE

    def tile(ref, h, g, base, offset=0):
        return ref[h, pl.ds(base + (g * SUBS + offset), SUBS), :]

    def get(ref, base, offset=0):
        return {(h, g): tile(ref, h, g, base, offset) for h, g in cells}

    def put(ref, base, values):
        for h, g in cells:
            ref[h, pl.ds(base + g * SUBS, SUBS), :] = values[h, g]

    def y_down(v):
        r = {c: pltpu.roll(v[c], 1, 0) for c in cells}
        return {(h, g): jnp.where(first_sub, r[h, g - 1], r[h, g]) if g > 0 else r[h, g]
                for h, g in cells}

    def z_up(v):
        r = {c: pltpu.roll(v[c], LANES - 1, 1) for c in v}
        return {(h, g): jnp.where(last_lane, r[h + 1, g], r[h, g]) if h < nh - 1 else r[h, g]
                for h, g in v}

    def z_down(v):
        r = {c: pltpu.roll(v[c], 1, 1) for c in v}
        return {(h, g): jnp.where(first_lane, r[h - 1, g], r[h, g]) if h > 0 else r[h, g]
                for h, g in v}

    flat = lambda v: tuple(v[c] for c in cells)
    dict_of = lambda t: dict(zip(cells, t))

    def coef_body(i, carry):
        here, cx_before = dict_of(carry[0]), dict_of(carry[1])
        for q in range(PLANES):
            low = pl.multiple_of((i * PLANES + q) * ny, ny)
            base = low + OFF
            after = get(kk, base + ny)
            up, right = get(kk, base, 1), z_up(here)
            fx = {c: (here[c] + after[c]) * sixteenth for c in cells}
            fy_ = {c: (here[c] + up[c]) * sixteenth for c in cells}
            fz = {c: (here[c] + right[c]) * sixteenth for c in cells}
            for h in halves:
                fy_[h, ng - 1] = jnp.where(last_sub, 0.0, fy_[h, ng - 1])
            for g in range(ng):
                fz[nh - 1, g] = jnp.where(last_lane, 0.0, fz[nh - 1, g])
            fyb, fzb = y_down(fy_), z_down(fz)
            for h in halves:
                fyb[h, 0] = jnp.where(first_sub, 0.0, fyb[h, 0])
            for g in range(ng):
                fzb[0, g] = jnp.where(first_lane, 0.0, fzb[0, g])
            total = {c: ((fx[c] + cx_before[c]) + (fy_[c] + fyb[c])) + (fz[c] + fzb[c])
                     for c in cells}
            for g in range(ng):
                total[0, g] = total[0, g] + jnp.where(first_lane, here[0, g] * sixteenth, 0.0)
                total[nh - 1, g] = total[nh - 1, g] + jnp.where(
                    last_lane, here[nh - 1, g] * sixteenth, 0.0)
            for ref, val in ((cx, fx), (cy, fy_), (cyb, fyb), (cz, fz), (czb, fzb), (diag, total)):
                put(ref, base, val)
            here, cx_before = after, fx
        return flat(here), flat(cx_before)

    lax.fori_loop(0, nx // PLANES, coef_body, (flat(get(kk, OFF)), (zero,) * len(cells)))
    last = OFF + count - ny
    put(diag, last, {c: tile(diag, *c, last) - tile(cx, *c, last) for c in cells})
    put(cx, last, {c: zero for c in cells})

    rows_in = [jnp.where((sub + g * SUBS >= 2) & (sub + g * SUBS < ny - 2), 1.0, 0.0).astype(F32)
               for g in range(ng)]

    def stencil(src, dst, shift, residual, pairs):
        def body(i, carry):
            here, before, cx_before = (dict_of(t) for t in carry[:3])
            accs = [list(t) for t in carry[3]]
            ends = {}
            if any(masked for _, _, masked in pairs):
                low_on = jnp.where(i > 0, 1.0, 0.0).astype(F32)
                high_on = jnp.where(i < nx // PLANES - 1, 1.0, 0.0).astype(F32)
                for q in (0, 1):
                    ends[q] = [m * low_on for m in rows_in]
                    ends[PLANES - 1 - q] = [m * high_on for m in rows_in]
            for q in range(PLANES):
                low = pl.multiple_of((i * PLANES + q) * ny, ny)
                base = low + OFF
                after = get(src, base + ny)
                up, down, right, left = get(src, base, 1), get(src, base, -1), z_up(here), z_down(here)
                new = {}
                fx = get(cx, base)
                for c in cells:
                    d = tile(diag, *c, base)
                    val = (d - shift if shift else d) * here[c]
                    val = val - fx[c] * after[c]
                    val = val - cx_before[c] * before[c]
                    val = val - tile(cy, *c, base) * up[c]
                    val = val - tile(cyb, *c, base) * down[c]
                    val = val - tile(cz, *c, base) * right[c]
                    val = val - tile(czb, *c, base) * left[c]
                    if residual:
                        val = tile(rs, *c, low) - SCALE * val
                    new[c] = val
                put(dst, base, new)
                known = {"here": here, "new": new}
                for h, g in cells:
                    mask = ends.get(q, rows_in)[g]
                    inside = {}
                    for acc, (one, two, masked) in zip(accs, pairs):
                        first_of, second_of = (
                            known[v][h, g] if isinstance(v, str) else tile(v, h, g, base)
                            for v in (one, two))
                        if masked:
                            if one not in inside:
                                inside[one] = first_of * mask
                            first_of = inside[one]
                        acc[h] = acc[h] + first_of * second_of
                before, here, cx_before = here, after, fx
            return flat(here), flat(before), flat(cx_before), tuple(tuple(a) for a in accs)
        nothing = (zero,) * len(cells)
        out = lax.fori_loop(0, nx // PLANES, body,
                            (flat(get(src, OFF)), nothing, nothing, ((zero,) * nh,) * len(pairs)))
        return [add_up(list(t)) for t in out[3]]

    for cp in loads[2 * nh:]:
        cp.wait()
    stencil(uu, w[0], 0.0, True, [])
    for side in range(2):
        for h in halves:
            for e, ref in ((3, cz), (4, czb), (5, cyb if side else cy), (1, cx)):
                own_y[side, e, h] = ref[h, strided(side), :]
            bump_y[h, along, :] = own_y[side, 1, h]
        for h in halves:
            own_y[side, 2, h] = bump_y[h, pl.ds(SUBS - 1, nx), :]
    arrive(first[4:])
    for side in range(2):
        at = plane_at(side)
        coef = (kk[:, at, :] + gxk[side]) * sixteenth
        cfx[side] = coef
        w[0][:, at, :] = w[0][:, at, :] - SCALE * (coef * (uu[:, at, :] - gxu[side]))
        diag[:, at, :] = diag[:, at, :] + coef
    arrive(first[:2])
    for side in range(2):
        for h in halves:
            coef = (fyk[side, h] + gyk[side, h]) * sixteenth
            cfy[side, h] = coef
            fyw[0, side, h] = w[0][h, strided(side), :] - SCALE * (coef * fyu[side, h])
            diag[h, strided(side), :] = diag[h, strided(side), :] + coef
    for side in range(2):
        for h in halves:
            own_y[side, 0, h] = diag[h, strided(side), :]
    arrive(first[2:4])
    for side in range(2):
        for h in halves:
            fyw[0, side, h] = fyw[0, side, h] + (SCALE * cfy[side, h]) * gyu[side, h]

    def send_near(r, ref):
        made = []
        for side in range(2):
            made.append(transfer(fyw.at[r, 1 - side], gyw.at[r, side], 0, toward(side)))
        for side in range(2):
            for h in halves:
                ref[h, strided(side), :] = fyw[r, side, h]
        for side in range(2):
            made.append(transfer(ref.at[:, plane_at(1 - side), :], gxw.at[r, side], toward(side), 0))
        return made, send_corners(ref, cw.at[r], gcw.at[r])

    def sideways(values, step):
        length = values[0].shape[0]
        index = lax.broadcasted_iota(jnp.int32, (length, LANES), 1)
        rolled = [pltpu.roll(v, LANES - 1 if step > 0 else 1, 1) for v in values]
        made = []
        for h in halves:
            if step > 0 and h < nh - 1:
                made.append(jnp.where(index == LANES - 1, rolled[h + 1], rolled[h]))
            elif step < 0 and h > 0:
                made.append(jnp.where(index == 0, rolled[h - 1], rolled[h]))
            else:
                made.append(rolled[h])
        return made

    def shifted_rows(ref, length, step):
        return [ref[h, pl.ds(SUBS + step, length), :] for h in halves]

    def in_plane(values, inside, shift, bump, length):
        for h in halves:
            bump[h, pl.ds(SUBS, length), :] = values[h]
        right, left = sideways(values, 1), sideways(values, -1)
        up, down = shifted_rows(bump, length, 1), shifted_rows(bump, length, -1)
        made = []
        for h in halves:
            total, fu, fd, fz, fzb = (inside(e, h) for e in range(5))
            val = (total - shift) * values[h] - fu * up[h] - fd * down[h]
            made.append(val - fz * right[h] - fzb * left[h])
        return made

    def x_coefs(side):
        at = plane_at(side)
        def inside(e, h):
            if e == 5:
                return cx[h, plane_at(side, 0 if side == 0 else 1), :]
            return (diag, cy, cyb, cz, czb)[e][h, at, :]
        return inside

    def y_coefs(side):
        return lambda e, h: own_y[side, e, h]

    there_c = [jnp.where(e, 0.0, 1.0).astype(F32) for e in edge_c]
    there_r = [jnp.where(e, 0.0, 1.0).astype(F32) for e in edge_r]

    def send_next(r, src, shift):
        made = []
        for side in range(2):
            within = [src[h, strided(side, 1), :] for h in halves]
            val = in_plane([fyw[r, side, h] for h in halves], y_coefs(side), shift, bump_y, nx)
            for h in halves:
                fyp[r, side, h] = val[h] - own_y[side, 5, h] * within[h]
                if r:
                    inner_y[side, h] = within[h]
        for side in range(2):
            made.append(transfer(fyp.at[r, 1 - side], gyp.at[r, side], 0, toward(side)))
        for side in range(2):
            at, below = plane_at(side), plane_at(side, 1)
            inside = x_coefs(side)
            val = in_plane([src[h, at, :] for h in halves], inside, shift, bump_x, ny)
            for h in halves:
                fxp[r, side, h] = val[h] - inside(5, h) * src[h, below, :]
        for side in range(2):
            made.append(transfer(fxp.at[r, 1 - side], gxp.at[r, side], toward(side), 0))
        return made

    def mend(mid, r):
        for side in range(2):
            at = plane_at(side)
            for h in halves:
                mid[h, at, :] = mid[h, at, :] + gxw[r, side, h]
        for side in range(2):
            for h in halves:
                new = mid[h, strided(side), :] + gyw[r, side, h]
                mid[h, strided(side), :] = new
                if r:
                    gyw[r, side, h] = new

    sums = {}
    for r in range(2):
        src, mid, dst = w[2 * r:2 * r + 3]
        shift_one, shift_two = NEWTON[2 * r] / SCALE, NEWTON[2 * r + 1] / SCALE
        near, corners = send_near(r, src)
        far = send_next(r, src, shift_one)
        if r == 0:
            sums[0, 0], = stencil(src, mid, shift_one, False, [("here", "here", False)])
            stencil(mid, dst, shift_two, False, [])
            arrive(second)
            for side in range(2):
                for end in range(2):
                    q = 2 * end + side
                    corner_y[side, end] = (gck[q] + gyk[side, :, pl.ds(end * (nx - 1), 1), :]) * sixteenth
                    q = 2 * side + end
                    corner_x[side, end] = (gck[q] + gxk[side, :, pl.ds(end * (ny - 1), 1), :]) * sixteenth
        else:
            mend(w[1], 0)
            sums[2, 2], sums[1, 2], sums[1, 1], sums[0, 1] = stencil(
                src, mid, shift_one, False,
                [("here", "here", False), ("here", w[1], False), (w[1], w[1], False),
                 (w[1], w[0], False)])
            last_four = stencil(
                mid, dst, shift_two, False,
                [("here", "here", True), ("here", w[2], True), ("new", "new", True),
                 ("new", "here", True)])
        near_y, near_x, far_y, far_x = near[:2], near[2:], far[:2], far[2:]
        arrive(near_y)
        for side in range(2):
            one = [-(cfy[side, h] * gyw[r, side, h]) for h in halves]
            two = in_plane(one, y_coefs(side), shift_two, bump_y, nx)
            for h in halves:
                gyw[r, side, h] = one[h]
                outer_y[side, h] = two[h]
        arrive(near_x)
        arrive(far_x)
        arrive(corners)
        for side in range(2):
            at, below = plane_at(side), plane_at(side, 1)
            inside = x_coefs(side)
            one = [-(cfx[side, h] * gxw[r, side, h]) for h in halves]
            two = in_plane(one, inside, shift_two, bump_x, ny)
            for end in range(2):
                row_at = pl.ds(end * (ny - 1), 1)
                gxp[r, side, :, row_at, :] = (
                    gxp[r, side, :, row_at, :] - corner_x[side, end] * gcw[r, 2 * side + end])
            for h in halves:
                gxw[r, side, h] = one[h]
                val = (gxp[r, side, h] - cfx[side, h] * src[h, at, :]) * there_r[side]
                dst[h, at, :] = dst[h, at, :] + (two[h] - cfx[side, h] * val)
                dst[h, below, :] = dst[h, below, :] - inside(5, h) * one[h]
        for side in range(2):
            one = [gyw[r, side, h] for h in halves]
            two = [outer_y[side, h] for h in halves]
            for h in halves:
                two_y[side, h] = cfy[side, h] * fyw[r, side, h]
            for end in range(2):
                row_at = pl.ds(end * (nx - 1), 1)
                two_y[side, :, row_at, :] = (
                    two_y[side, :, row_at, :] + corner_y[side, end] * gcw[r, 2 * end + side])
            for h in halves:
                weight = cfy[side, h] * there_c[side]
                outer_y[side, h] = dst[h, strided(side), :] + (two[h] + weight * two_y[side, h])
                within = dst[h, strided(side, 1), :] - own_y[side, 5, h] * one[h]
                dst[h, strided(side, 1), :] = within
                two_y[side, h] = within
        arrive(far_y)
        for side in range(2):
            for h in halves:
                outer = outer_y[side, h] - (cfy[side, h] * there_c[side]) * gyp[r, side, h]
                if r == 0:
                    fyw[1, side, h] = outer
                else:
                    dst[h, strided(side), :] = outer
                    outer_y[side, h] = outer
    mend(w[3], 1)

    def fold(values):
        return jnp.sum(values.reshape(-1, SUBS, LANES), axis=0)

    row = lax.broadcasted_iota(jnp.int32, (nx, LANES), 0)
    planes_in = (row >= 2) & (row < nx - 2)
    for side in range(2):
        for h in halves:
            for two_at, three_at, four_at in (
                    (fyw[1, side, h], gyw[1, side, h], outer_y[side, h]),
                    (inner_y[side, h], w[3][h, strided(side, 1), :], two_y[side, h])):
                third = jnp.where(planes_in, three_at, 0.0)
                fourth = jnp.where(planes_in, four_at, 0.0)
                for e, val in enumerate((third * three_at, third * two_at,
                                         fourth * four_at, fourth * three_at)):
                    last_four[e] = last_four[e] + fold(val)
            for depth in range(2):
                at = plane_at(side, depth)
                two_at, three_at, four_at = (w[k][h, at, :] for k in (2, 3, 4))
                for e, val in enumerate((three_at * three_at, three_at * two_at,
                                         four_at * four_at, four_at * three_at)):
                    last_four[e] = last_four[e] + fold(val)
    sums[3, 3], sums[2, 3], sums[4, 4], sums[3, 4] = last_four


    def exchange(buf, ssem, rsem, peers, value):
        here = len(peers)
        buf[here] = value
        for e, (dr, dc) in enumerate(peers):
            pltpu.make_async_remote_copy(
                src_ref=buf.at[here], dst_ref=buf.at[e], send_sem=ssem.at[0], recv_sem=rsem.at[0],
                device_id=device(dr, dc), device_id_type=MESH).start()
        while sent:
            has_target, copy = sent.pop()

            @pl.when(has_target)
            def _(copy=copy):
                copy.wait_send()
        whole = buf.at[pl.ds(0, here)]
        pltpu.make_async_copy(whole, whole, rsem.at[0]).wait()
        parts = [buf[i] for i in range(here + 1)]
        while len(parts) > 1:
            parts = [a + b for a, b in zip(parts[::2], parts[1::2])] + (
                parts[-1:] if len(parts) % 2 else [])
        return parts[0]

    def finish_sends(buf, ssem, peers):
        whole = buf.at[pl.ds(0, len(peers))]
        pltpu.make_async_copy(whole, whole, ssem.at[0]).wait()

    everyone = [(dr, dc) for dr in range(nrows) for dc in range(ncols)][1:]
    pair_row = lax.broadcasted_iota(jnp.int32, (16, LANES), 0)
    on_diag = pair_row == lax.broadcasted_iota(jnp.int32, (16, LANES), 1)
    gm[...] = jnp.zeros(gm.shape, F32)
    for e, pair in enumerate(SUMS):
        gm[e:e + 1, :] = jnp.sum(sums[pair], axis=0, keepdims=True)
    line = jnp.sum(jnp.where(on_diag, jnp.sum(gm[...], axis=1, keepdims=True), 0.0),
                   axis=0, keepdims=True)
    if one_stage:
        pl.semaphore_wait(in_sem, len(row_peers))
        line = exchange(g1, s1, r1, everyone, line)
    else:
        line = exchange(g1, s1, r1, col_peers, line)
        line = exchange(g2, s2, r2, row_peers, line)
    gm[...] = jnp.broadcast_to(
        jnp.sum(jnp.where(on_diag, line, 0.0), axis=1, keepdims=True), gm.shape)
    moments = {pair: gm[e:e + 1, :] for e, pair in enumerate(SUMS)}
    for gap in range(2, 5):
        for i in range(5 - gap):
            j = i + gap
            moments[i, j] = moments[i + 1, j - 1] + (
                (NEWTON[i] - NEWTON[j - 1]) / SCALE) * moments[i, j - 1]
            moments[i, j] = moments[i, j]
    gram_one = lambda i, j: moments[min(i, j), max(i, j)]
    low_one, inv_one = cholesky(gram_one, 5)
    linv_one = lower_inverse(low_one, inv_one, 5)
    half = {(i, j): add_up([linv_one[i, m] * gram_one(m, j) for m in range(i + 1)])
            for i in range(5) for j in range(i + 1)}
    gram_two = {(i, j): add_up([half[i, m] * linv_one[j, m] for m in range(j + 1)])
                for i in range(5) for j in range(i + 1)}
    low_two, inv_two = cholesky(lambda i, j: gram_two[i, j], 5)
    linv_two = lower_inverse(low_two, inv_two, 5)

    trans = {(i, j): add_up([linv_two[i, m] * linv_one[m, j] for m in range(j, i + 1)])
             for i in range(5) for j in range(i + 1)}
    rfac = {(i, j): add_up([low_two[m, i] * low_one[j, m] for m in range(i, j + 1)])
            for i in range(5) for j in range(i, 5)}
    shifted = {}
    for k in range(4):
        for i in range(k + 2):
            val = rfac[i, k + 1] * SCALE
            shifted[i, k] = val + rfac[i, k] * NEWTON[k] if i <= k else val
    hess = {(i, k): add_up([shifted[i, m] * trans[k, m] for m in range(max(i - 1, 0), k + 1)])
            for k in range(4) for i in range(k + 2)}
    target, inv_n = [rfac[0, 0]], []
    for k in range(4):
        top, bottom = hess[k, k], hess[k + 1, k]
        square = top * top + bottom * bottom
        inv_n.append(inv_sqrt(square))
        cosine, sine = top * inv_n[k], bottom * inv_n[k]
        for j in range(k + 1, 4):
            upper, under = hess[k, j], hess[k + 1, j]
            hess[k, j] = cosine * upper + sine * under
            hess[k + 1, j] = cosine * under - sine * upper
        target.append(-(sine * target[k]))
        target[k] = cosine * target[k]
    weights = [None] * 4
    for i in range(3, -1, -1):
        val = target[i]
        for m in range(i + 1, 4):
            val = val - hess[i, m] * weights[m]
        weights[i] = val * inv_n[i]

    root = math.sqrt(nrows * ncols * nx * ny * nz)
    for e, (j, i) in enumerate(PAIRS):
        coef_out[e:e + 1, :] = trans[i, j] * root
    for k in range(4):
        coef_out[16 + k:17 + k, :] = weights[k] * (1.0 / root)
    one_row = lax.broadcasted_iota(jnp.int32, (1, LANES), 1)
    for i in range(5):
        line = jnp.zeros((1, LANES), F32)
        column = [rfac[i, 0] if i == 0 else jnp.zeros((1, LANES), F32)]
        for j in range(1, 5):
            below = rfac[i, j] if j >= i else 0.0
            column.append(below - column[j - 1] * (SHIFTS[j - 1] / SCALE))
        for j in range(i, 5):
            line = jnp.where(one_row == j, column[j], line)
        coef_out[24 + i:25 + i, :] = line

    if one_stage:
        finish_sends(g1, s1, everyone)
    else:
        finish_sends(g1, s1, col_peers)
        finish_sends(g2, s2, row_peers)


def finish_kernel(parts, nz, w_ref, coef_ref, basis_hbm, rfac_ref, updated_hbm, stage, last, sems):
    trans = {(i, j): jnp.broadcast_to(coef_ref[e:e + 1, :], (SUBS, LANES))
             for e, (j, i) in enumerate(PAIRS)}
    weights = [jnp.broadcast_to(coef_ref[16 + k:17 + k, :], (SUBS, LANES)) for k in range(4)]
    rfac_ref[...] = coef_ref[24:29, 0:5]
    copies = []
    for part, (start, size) in enumerate(parts):

        def body(n, carry):
            low = pl.multiple_of(start + n * SUBS, SUBS)
            at, rows_in = pl.ds(low, SUBS), pl.ds(low + OFF, SUBS)
            for h in range(nz // LANES):
                lanes = pl.ds(h * LANES, LANES)
                raw = [w_ref[k, h, rows_in, :] for k in range(5)]
                new = w_ref[5, h, rows_in, :]
                for i in range(5):
                    val = trans[i, 0] * raw[0]
                    for j in range(1, i + 1):
                        val = val + trans[i, j] * raw[j]
                    stage[i, at, lanes] = val
                    if i < 4:
                        new = new + weights[i] * val
                last[at, lanes] = new
            return carry
        lax.fori_loop(0, size // SUBS, body, 0, unroll=8)
        rows = pl.ds(start, size)
        for e, (src, dst) in enumerate(((stage.at[:, rows, :], basis_hbm.at[:, rows, :]),
                                        (last.at[rows, :], updated_hbm.at[rows, :]))):
            copies.append(pltpu.make_async_copy(src, dst, sems.at[part, e]))
            copies[-1].start()
    for copy in copies:
        copy.wait()


def on_device(nrows, ncols, right_side, initial, conduct):
    nx, ny, nz = initial.shape
    nh, count = nz // LANES, nx * ny
    flat = [a.reshape(count, nz) for a in (right_side, initial, conduct)]
    dma = pltpu.SemaphoreType.DMA
    slots = nrows * ncols if nrows * ncols <= 64 else ncols
    field = pltpu.VMEM((nh, count, LANES), F32)
    padded = pltpu.VMEM((nh, OFF + count + ny, LANES), F32)
    ends = 2 * SUBS
    y_pair, x_pair = pltpu.VMEM((2, nh, nx, LANES), F32), pltpu.VMEM((2, nh, ny, LANES), F32)
    y_four, x_four = pltpu.VMEM((2, 2, nh, nx, LANES), F32), pltpu.VMEM((2, 2, nh, ny, LANES), F32)
    vectors, coefs = pl.pallas_call(
        functools.partial(cycle_kernel, (nrows, ncols, nx, ny, nz)),
        out_shape=(pltpu.VMEM((6, nh, OFF + count + ny, LANES), F32),
                   pltpu.VMEM((32, LANES), F32)),
        in_specs=[pl.BlockSpec(memory_space=pltpu.HBM)] * 3,
        out_specs=(pl.BlockSpec(memory_space=pltpu.VMEM), pl.BlockSpec(memory_space=pltpu.VMEM)),
        scratch_shapes=[
            padded, field, padded, padded, padded, padded, padded, padded,
            pltpu.VMEM((2, nh, ny, LANES), F32), pltpu.VMEM((2, nh, nx, LANES), F32),
            y_pair, y_pair, y_four, y_four, x_four, y_pair, y_pair, y_four, y_four,
            x_pair, x_pair, x_four, x_four,
            pltpu.VMEM((4, nh, 1, LANES), F32), pltpu.VMEM((2, 4, nh, 1, LANES), F32),
            pltpu.VMEM((4, nh, 1, LANES), F32), pltpu.VMEM((2, 4, nh, 1, LANES), F32),
            pltpu.VMEM((2, 2, nh, 1, LANES), F32), pltpu.VMEM((2, 2, nh, 1, LANES), F32),
            pltpu.VMEM((2, 6, nh, nx, LANES), F32), y_pair, y_pair, y_pair,
            pltpu.VMEM((nh, nx + ends, LANES), F32), pltpu.VMEM((nh, ny + ends, LANES), F32),
            pltpu.VMEM((slots, 1, LANES), F32), pltpu.VMEM((nrows, 1, LANES), F32),
            pltpu.VMEM((16, LANES), F32),
            dma((3, nh)), dma((36,)), dma((36,)),
            dma((1,)), dma((1,)), dma((1,)), dma((1,)), pltpu.SemaphoreType.REGULAR,
        ],
        compiler_params=pltpu.CompilerParams(
            collective_id=0, has_side_effects=True, vmem_limit_bytes=57 << 20),
        name="cycle",
    )(*flat)
    unit = count // 16
    sizes = [unit * n for n in (1, 3, 4, 4, 3, 1)]
    parts = [(sum(sizes[:i]), size) for i, size in enumerate(sizes)]
    basis, rfactor, updated = pl.pallas_call(
        functools.partial(finish_kernel, parts, nz),
        out_shape=(jax.ShapeDtypeStruct((5, count, nz), F32),
                   jax.ShapeDtypeStruct((5, 5), F32),
                   jax.ShapeDtypeStruct((count, nz), F32)),
        in_specs=[pl.BlockSpec(memory_space=pltpu.VMEM)] * 2,
        out_specs=(pl.BlockSpec(memory_space=pltpu.HBM), pl.BlockSpec(memory_space=pltpu.VMEM),
                   pl.BlockSpec(memory_space=pltpu.HBM)),
        scratch_shapes=[pltpu.VMEM((5, count, nz), F32), pltpu.VMEM((count, nz), F32),
                        dma((len(parts), 2))],
        compiler_params=pltpu.CompilerParams(vmem_limit_bytes=20 << 20),
        name="finish",
    )(vectors, coefs)
    return (basis.reshape(5, nx, ny, nz), rfactor, updated.reshape(nx, ny, nz))


def solution(mesh):
    nrows, ncols = mesh.shape["rows"], mesh.shape["cols"]
    return jax.shard_map(
        functools.partial(on_device, nrows, ncols),
        mesh=mesh,
        in_specs=(P("rows", "cols", None),) * 3,
        out_specs=(P(None, "rows", "cols", None), P(), P("rows", "cols", None)),
        check_vma=False,
    )
```
